512 devices in a mesh: pipe: 8 (over y, core), ctx: 32 (over x, z_lo), tp: 2 (over z_hi).
Axes of the slice: x: 4, y: 4, z: 16 (z_hi: 2, z_lo: 8; z = z_hi * 8 + z_lo), core: 2. Of those that a mesh axis runs over, the one named last changes fastest.
Arguments:
- stream: bfloat16 [8, 4096, 4096], P('pipe', 'ctx', 'tp'), may hold values from -6 to 6
- queries: bfloat16 [8, 4096, 4096], P('pipe', 'ctx', 'tp'), may hold values from -5 to 5
- keys: bfloat16 [8, 4096, 1024], P('pipe', 'ctx', 'tp'), may hold values from -5 to 5
- values: bfloat16 [8, 4096, 1024], P('pipe', 'ctx', 'tp'), may hold values from -6 to 6
- segments: int32 [8, 4096], P('pipe', 'ctx'), may hold values from 0 to 5, never falling along the last dimension, each value on 1 to 2048 neighbouring positions
- norm_gain: bfloat16 [4096], P('tp'), may hold values from 0.25 to 1.75
Outputs:
- arrived: bfloat16 [8, 4096, 4096], P('pipe', 'ctx', 'tp')
- normed: bfloat16 [8, 4096, 4096], P('pipe', 'ctx', 'tp')
The draws below stay inside these ranges and needn't reach their ends.
Inputs may be any that keep to these rules, and one draw needn't show every extreme that they name: `segments`: in each section's micro-batch the document number never falls along positions; each document holds 1 to half of 4096 positions, and one holds exactly half of 4096.
All inputs are finite; a program needn't handle non-finite values.
Results may differ from the reference program's by a relative error of at most 0.006.
Values may be sent and summed in bfloat16 or wider, within the bound.
A program may use at most 128 MiB of HBM per device.

```python
import math
import jax
import jax.numpy as jnp
import numpy as np
from jax import lax

QUERY_HEADS = 32
KEY_VALUE_HEADS = 8
HEAD_SIZE = 128
DOCS = 6
TOK_DEV = 128
RELAY_SECTIONS = 8
MICRO_POSITIONS = 4096
N_CTX = 32


def unsigned_entries(key, width):
    return jax.random.truncated_normal(key, -5.0, 5.0, (RELAY_SECTIONS, MICRO_POSITIONS, width), jnp.float32)


def draw_queries(key, part):
    table_entries = unsigned_entries(jax.random.fold_in(key, 11), QUERY_HEADS * HEAD_SIZE)
    return table_entries.astype(jnp.bfloat16)


def draw_keys(key, part):
    table_entries = unsigned_entries(jax.random.fold_in(key, 13), KEY_VALUE_HEADS * HEAD_SIZE)
    return table_entries.astype(jnp.bfloat16)


def level_of(own_key, extent, shards, smallest, largest):
    factor_of, own = 1.0, jax.random.fold_in(own_key, 6)
    for axis_at, parts in shards:
        steps = jnp.exp(jax.random.uniform(jax.random.fold_in(own, axis_at), (parts,), jnp.float32, smallest / len(shards), largest / len(shards)))
        factor_of = factor_of * jnp.repeat(steps, extent[axis_at] // parts).reshape([-1 if axis == axis_at else 1 for axis in range(len(extent))])
    return factor_of


def length_profile(amount, total, limit, slope):
    loads = [(1 << 20) // math.isqrt(rank ** slope) + 1 for rank in range(2, amount + 1)]
    rest, given = total - limit - (amount - 1), [1] * (amount - 1)
    while rest > 0:
        candidates = [i for i in range(amount - 1) if given[i] < limit]
        mass, left = sum([loads[i] for i in candidates]), rest
        for i in candidates:
            extra = min(limit - given[i], max(1, left * loads[i] // mass), rest)
            given[i] = given[i] + extra
            rest = rest - extra
    return np.array([limit] + given)


def uneven_parts(stream_key, number_of, total, bound, slope):
    if number_of == 2:
        one = jax.random.randint(stream_key, (), max(1, total - bound), min(bound, total - 1) + 1)
        return jnp.stack([one, total - one])
    sizes = jnp.asarray(length_profile(number_of, total, bound, slope), jnp.int32)
    couples = (number_of - 1) // 2
    giver, receiver = sizes[1:1 + 2 * couples:2], sizes[2:2 + 2 * couples:2]
    room = jnp.minimum(giver - 1, bound - receiver)
    shifted = jax.random.randint(jax.random.fold_in(stream_key, 1), (couples,), 0, 1 << 20) % (room + 1)
    sizes = sizes.at[1:1 + 2 * couples:2].set(giver - shifted).at[2:2 + 2 * couples:2].set(receiver + shifted)
    return sizes[jax.random.permutation(jax.random.fold_in(stream_key, 2), number_of)]


def centred(stream_key, dims, scale, limit, cuts=(), kind=jnp.bfloat16):
    loudness = level_of(stream_key, dims, cuts, -0.22, 0.18) if cuts else 1.0
    values = jax.random.normal(stream_key, dims, jnp.float32) * scale * loudness
    return jnp.minimum(jnp.maximum(values, -limit), limit).astype(kind)


def setup_inputs(seed: int = 0) -> dict:
    splits = jax.random.split(jax.random.key(seed), 7)
    return {
        "stream": centred(splits[0], (RELAY_SECTIONS, MICRO_POSITIONS, QUERY_HEADS * HEAD_SIZE), 1.0, 6.0, ((0, 8), (1, 32), (2, 2))),
        "queries": draw_queries(jax.random.fold_in(splits[6], 71), 0),
        "keys": draw_keys(jax.random.fold_in(splits[6], 71), 0),
        "values": centred(splits[3], (RELAY_SECTIONS, MICRO_POSITIONS, KEY_VALUE_HEADS * HEAD_SIZE), 1.0, 6.0, ((0, 8), (1, 32), (2, 2))),
        "segments": jax.vmap(lambda own: jnp.searchsorted(jnp.cumsum(uneven_parts(own, DOCS, MICRO_POSITIONS, TOK_DEV * N_CTX // 2, 2)), jnp.arange(MICRO_POSITIONS), side="right"))(jax.random.split(splits[4], RELAY_SECTIONS)).reshape((RELAY_SECTIONS, MICRO_POSITIONS)).astype(jnp.int32),
        "norm_gain": jnp.clip(1.0 + 0.15 * jax.random.normal(splits[5], (QUERY_HEADS * HEAD_SIZE,), jnp.float32), 0.25, 1.75).astype(jnp.bfloat16),
    }


def attend_section(query_row_block, key_row_block, value_row_block, seg_ids):
    span_length = query_row_block.shape[0]
    query_group_size = QUERY_HEADS // KEY_VALUE_HEADS
    span = math.gcd(span_length, 512)
    score_scale = HEAD_SIZE ** (-0.5)
    positions = jnp.arange(span_length, dtype=jnp.int32)
    query_head_stack = query_row_block.reshape(span_length, KEY_VALUE_HEADS, query_group_size, HEAD_SIZE).transpose(1, 2, 0, 3)
    key_head_stack = key_row_block.reshape(span_length, KEY_VALUE_HEADS, HEAD_SIZE).transpose(1, 0, 2)
    value_head_stack = value_row_block.reshape(span_length, KEY_VALUE_HEADS, HEAD_SIZE).transpose(1, 0, 2)

    def per_head(operands):
        query_head, key_head, value_head = operands
        key_wide = key_head.astype(jnp.float32)
        value_wide = value_head.astype(jnp.float32)

        def per_block(row_start):
            query_block = lax.dynamic_slice_in_dim(query_head, row_start, span, 1).astype(jnp.float32)
            query_pos = row_start + jnp.arange(span, dtype=jnp.int32)
            query_seg = lax.dynamic_slice_in_dim(seg_ids, row_start, span, 0)
            scores = jnp.einsum('gqd,kd->gqk', query_block, key_wide) * score_scale
            allowed = (positions[None, :] <= query_pos[:, None]) & (seg_ids[None, :] == query_seg[:, None])
            scores = jnp.where(allowed[None], scores, -jnp.inf)
            top = lax.optimization_barrier(jnp.max(scores, axis=-1, keepdims=True))
            weights = jnp.where(allowed[None], jnp.exp(scores - top), 0.0)
            total = lax.optimization_barrier(jnp.sum(weights, axis=-1, keepdims=True))
            rounded = lax.optimization_barrier(weights.astype(jnp.bfloat16)).astype(jnp.float32)
            mixed = jnp.einsum('gqk,kd->gqd', rounded, value_wide) / total
            return mixed.astype(jnp.bfloat16)
        starts = jnp.arange(0, span_length, span, dtype=jnp.int32)
        blocks = lax.map(per_block, starts)
        return blocks.transpose(1, 0, 2, 3).reshape(query_group_size, span_length, HEAD_SIZE)
    heads_out = lax.map(per_head, (query_head_stack, key_head_stack, value_head_stack))
    return heads_out.transpose(2, 0, 1, 3).reshape(span_length, QUERY_HEADS * HEAD_SIZE)

def reference(stream, queries, keys, values, segments, norm_gain):
    advanced_list = []
    for section in range(stream.shape[0]):
        attended = attend_section(queries[section], keys[section], values[section], segments[section])
        attended = lax.optimization_barrier(attended).astype(jnp.float32)
        advanced_list.append((stream[section].astype(jnp.float32) + attended).astype(jnp.bfloat16))
    advanced = jnp.stack(advanced_list)
    arrived = jnp.roll(advanced, 1, axis=0)
    wide = arrived.astype(jnp.float32)
    mean_square = lax.optimization_barrier(jnp.mean(wide * wide, axis=-1, keepdims=True))
    normed = (wide * lax.rsqrt(mean_square + 1e-05) * norm_gain.astype(jnp.float32)).astype(jnp.bfloat16)
    return (arrived, normed)
```

```python
import functools

import jax
import jax.numpy as jnp
from jax import lax
from jax.experimental import pallas as pl
from jax.experimental.pallas import tpu as pltpu
from jax.sharding import PartitionSpec as P

QUERY_HEADS = 32
HEAD = 128
MESH = pl.DeviceIdType.MESH
NZ = 8
OH_ROWS = 16
FAR = float(2**20)
LOG2E = 1.4426950408889634


def attention_kernel(
    kv_heads,
    group,
    q_ref,
    k_ref,
    v_ref,
    seg_ref,
    stream_ref,
    out_ref,
    qa,
    own,
    buf,
    m_ref,
    acc,
    recv_sem,
    sendz_sem,
    sendx_sem,
):
    rows = q_ref.shape[0]
    ctx = lax.axis_index("ctx")
    n_ctx = lax.axis_size("ctx")
    x = ctx // NZ
    z = ctx % NZ
    right = (ctx + NZ) % n_ctx
    left = (ctx + n_ctx - NZ) % n_ctx

    barrier = pltpu.get_barrier_semaphore()
    for peer in (right, left):
        pl.semaphore_signal(barrier, inc=1, device_id={"ctx": peer}, device_id_type=MESH)

    @pl.when(z < NZ - 1)
    def _():
        pl.semaphore_signal(barrier, inc=1, device_id={"ctx": ctx + 1}, device_id_type=MESH)

    @pl.when(z > 0)
    def _():
        pl.semaphore_signal(barrier, inc=1, device_id={"ctx": ctx - 1}, device_id_type=MESH)

    seg_f = seg_ref[...].astype(jnp.float32)
    doc_rows = lax.broadcasted_iota(jnp.int32, (OH_ROWS, rows), 0).astype(jnp.float32)
    own[0:OH_ROWS, :] = jnp.where(
        doc_rows == jnp.broadcast_to(seg_f, (OH_ROWS, rows)), 1.0, 0.0
    ).astype(jnp.bfloat16)
    for h in range(kv_heads):
        base = OH_ROWS + 2 * HEAD * h
        key_block = k_ref[:, h * HEAD : (h + 1) * HEAD].astype(jnp.float32)
        own[base : base + HEAD, :] = key_block.T.astype(jnp.bfloat16)
        own[base + HEAD : base + 2 * HEAD, :] = v_ref[:, h * HEAD : (h + 1) * HEAD]

    def part(h):
        if h == 0:
            return pl.ds(0, OH_ROWS + 2 * HEAD)
        return pl.ds(OH_ROWS + 2 * HEAD * h, 2 * HEAD)

    def copy_of(src, slot, which, h, sems, sem_row, peer):
        return pltpu.make_async_remote_copy(
            src_ref=src.at[part(h), :],
            dst_ref=buf.at[slot, which, part(h), :],
            send_sem=sems.at[sem_row, h],
            recv_sem=recv_sem.at[slot, which, h],
            device_id={"ctx": peer},
            device_id_type=MESH,
        )

    pl.semaphore_wait(barrier, 2 + jnp.where(z < NZ - 1, 1, 0) + jnp.where(z > 0, 1, 0))

    def up(h):
        return copy_of(own, z, 0, h, sendz_sem, NZ, ctx + 1)

    def across(h):
        return copy_of(own, z, 0, h, sendx_sem, NZ, right)

    for h in range(kv_heads):
        across(h).start()

        @pl.when(z < NZ - 1)
        def _():
            up(h).start()

    seg_col = jnp.broadcast_to(seg_f, (rows, rows)).T
    lane = lax.broadcasted_iota(jnp.int32, (rows, HEAD), 1)
    penalty = jnp.where(
        (lane < OH_ROWS) & (lane.astype(jnp.float32) != seg_col), -FAR, 0.0
    ).astype(jnp.bfloat16)
    for h in range(kv_heads):
        for g in range(group):
            c = (h * group + g) * HEAD
            qa[h, g * rows : (g + 1) * rows, 0:HEAD] = q_ref[:, c : c + HEAD]
            qa[h, g * rows : (g + 1) * rows, HEAD : 2 * HEAD] = penalty

    scale = LOG2E * HEAD ** (-0.5)
    height = group * rows
    ones = jnp.ones((2 * rows, HEAD), jnp.bfloat16)
    pad = jnp.zeros((HEAD - OH_ROWS, 2 * rows), jnp.bfloat16)

    causal = lax.broadcasted_iota(jnp.int32, (height, rows), 0) % rows >= lax.broadcasted_iota(
        jnp.int32, (height, rows), 1
    )
    for h in range(kv_heads):
        base = OH_ROWS + 2 * HEAD * h
        rhs = jnp.concatenate(
            [own[base : base + HEAD, :], own[0:OH_ROWS, :], pad[:, 0:rows]], axis=0
        )
        s = jnp.dot(qa[h], rhs, preferred_element_type=jnp.float32)
        s = jnp.where(causal, s, -FAR)
        top = jnp.broadcast_to(jnp.max(s, axis=1, keepdims=True), (height, HEAD))
        p = jnp.exp2((s - top) * scale).astype(jnp.bfloat16)
        va = jnp.concatenate([own[base + HEAD : base + 2 * HEAD, :], ones[0:rows]], axis=1)
        m_ref[h] = top
        acc[h] = jnp.dot(p, va, preferred_element_type=jnp.float32)

    nowhere = jnp.where(
        lax.broadcasted_iota(jnp.int32, (OH_ROWS, rows), 0) == OH_ROWS - 1, 1.0, 0.0
    ).astype(jnp.bfloat16)

    def slot_of(r, k):
        return (1 - k) * (z - r) + k * (z + r - 1)

    def exists(r, k):
        return r <= (1 - k) * z + k * (NZ - z)

    def forward_z(slot, k, h):
        return copy_of(buf.at[slot, 0], slot, 0, h, sendz_sem, slot, ctx + 1 - 2 * k)

    def forward_x(slot, h):
        return copy_of(buf.at[slot, 0], slot, 1, h, sendx_sem, slot, right)

    def has_next(k):
        return (1 - k) * (NZ - 1 - z) + k * z > 0

    def relay(r):
        def one(k, carry):
            @pl.when(exists(r, k))
            def _():
                slot = slot_of(r, k)
                for h in range(kv_heads):
                    copy_of(buf.at[slot, 0], slot, 0, h, sendz_sem, slot, right).wait_recv()

                    @pl.when(has_next(k))
                    def _():
                        forward_z(slot, k, h).start()

                    forward_x(slot, h).start()

            return carry

        lax.fori_loop(0, 2, one, 0)

    def attend(r):
        def one(k, carry):
            @pl.when(exists(r, k))
            def _():
                slot = slot_of(r, k)
                for h in range(kv_heads):
                    forward_x(slot, h).wait_recv()
                known0 = x >= k
                known1 = x >= k + 1
                oh0 = jnp.where(known0, buf[slot, 0, 0:OH_ROWS, :], nowhere)
                oh1 = jnp.where(known1, buf[slot, 1, 0:OH_ROWS, :], nowhere)
                oh = jnp.concatenate([oh0, oh1], axis=1)
                for h in range(kv_heads):
                    base = OH_ROWS + 2 * HEAD * h
                    kt = jnp.concatenate(
                        [buf[slot, 0, base : base + HEAD, :], buf[slot, 1, base : base + HEAD, :]],
                        axis=1,
                    )
                    rhs = jnp.concatenate([kt, oh, pad], axis=0)
                    s = jnp.dot(qa[h], rhs, preferred_element_type=jnp.float32)
                    old = m_ref[h]
                    top = jnp.maximum(old, jnp.max(s, axis=1, keepdims=True))
                    p = jnp.exp2((s - jnp.concatenate([top, top], axis=1)) * scale)
                    fade = jnp.exp2((old - top) * scale)
                    vals = jnp.concatenate(
                        [
                            buf[slot, 0, base + HEAD : base + 2 * HEAD, :],
                            buf[slot, 1, base + HEAD : base + 2 * HEAD, :],
                        ],
                        axis=0,
                    )
                    va = jnp.concatenate([vals, ones], axis=1)
                    m_ref[h] = top
                    acc[h] = acc[h] * jnp.concatenate([fade, fade], axis=1) + jnp.dot(
                        p.astype(jnp.bfloat16), va, preferred_element_type=jnp.float32
                    )

            return carry

        lax.fori_loop(0, 2, one, 0)

    def step(r, carry):
        relay(r)

        @pl.when(r > 1)
        def _():
            attend(r - 1)

        return carry

    lax.fori_loop(1, NZ + 1, step, 0)
    attend(NZ)

    for h in range(kv_heads):
        for g in range(group):
            c = (h * group + g) * HEAD
            top_rows = slice(g * rows, (g + 1) * rows)
            mixed = acc[h, top_rows, 0:HEAD] / acc[h, top_rows, HEAD : 2 * HEAD]
            mixed = mixed.astype(jnp.bfloat16).astype(jnp.float32)
            out_ref[:, c : c + HEAD] = (
                stream_ref[:, c : c + HEAD].astype(jnp.float32) + mixed
            ).astype(jnp.bfloat16)

    for h in range(kv_heads):
        across(h).wait_send()

        @pl.when(z < NZ - 1)
        def _():
            up(h).wait_send()

    def drain(r, carry):
        def one(k, inner):
            @pl.when(exists(r, k))
            def _():
                slot = slot_of(r, k)
                for h in range(kv_heads):
                    forward_x(slot, h).wait_send()

                    @pl.when(has_next(k))
                    def _():
                        forward_z(slot, k, h).wait_send()

            return inner

        lax.fori_loop(0, 2, one, 0)
        return carry

    lax.fori_loop(1, NZ + 1, drain, 0)


def attend_and_add(stream, queries, keys, values, segments):
    rows = queries.shape[0]
    kv_heads = keys.shape[1] // HEAD
    group = queries.shape[1] // keys.shape[1]
    block_rows = OH_ROWS + 2 * HEAD * kv_heads
    vmem = pl.BlockSpec(memory_space=pltpu.VMEM)
    return pl.pallas_call(
        functools.partial(attention_kernel, kv_heads, group),
        out_shape=jax.ShapeDtypeStruct(stream.shape, jnp.bfloat16),
        in_specs=[vmem] * 5,
        out_specs=vmem,
        scratch_shapes=[
            pltpu.VMEM((kv_heads, group * rows, 2 * HEAD), jnp.bfloat16),
            pltpu.VMEM((block_rows, rows), jnp.bfloat16),
            pltpu.VMEM((NZ, 2, block_rows, rows), jnp.bfloat16),
            pltpu.VMEM((kv_heads, group * rows, HEAD), jnp.float32),
            pltpu.VMEM((kv_heads, group * rows, 2 * HEAD), jnp.float32),
            pltpu.SemaphoreType.DMA((NZ, 2, kv_heads)),
            pltpu.SemaphoreType.DMA((NZ + 1, kv_heads)),
            pltpu.SemaphoreType.DMA((NZ + 1, kv_heads)),
        ],
        compiler_params=pltpu.CompilerParams(
            collective_id=0, has_side_effects=True, vmem_limit_bytes=48 * 1024 * 1024
        ),
    )(queries, keys, values, segments, stream)


def per_device(stream, queries, keys, values, segments, norm_gain):
    advanced = attend_and_add(stream[0], queries[0], keys[0], values[0], segments)
    n_pipe = lax.axis_size("pipe")
    arrived = lax.ppermute(
        advanced[None], "pipe", [((i - 1) % n_pipe, i) for i in range(n_pipe)]
    )
    wide = arrived.astype(jnp.float32)
    squares = jnp.sum(wide * wide, axis=-1)
    totals = lax.psum(squares, "tp")
    inverse = lax.rsqrt(totals / (QUERY_HEADS * HEAD) + 1e-05)
    normed = (wide * inverse[..., None] * norm_gain.astype(jnp.float32)).astype(jnp.bfloat16)
    return (arrived, normed)


def solution(mesh):
    in_specs = (
        P("pipe", "ctx", "tp"),
        P("pipe", "ctx", "tp"),
        P("pipe", "ctx", "tp"),
        P("pipe", "ctx", "tp"),
        P("pipe", "ctx"),
        P("tp"),
    )
    out_specs = (P("pipe", "ctx", "tp"), P("pipe", "ctx", "tp"))
    return jax.shard_map(
        per_device, mesh=mesh, in_specs=in_specs, out_specs=out_specs, check_vma=False
    )
```

```python
import functools

import jax
import jax.numpy as jnp
from jax import lax
from jax.experimental import pallas as pl
from jax.experimental.pallas import tpu as pltpu
from jax.sharding import PartitionSpec as P

QUERY_HEADS = 32
HEAD = 128
MESH = pl.DeviceIdType.MESH
NZ = 8
OH_ROWS = 16
FAR = float(2**20)
LOG2E = 1.4426950408889634


def attention_kernel(
    kv_heads,
    group,
    q_hbm,
    k_hbm,
    v_hbm,
    stream_hbm,
    seg_ref,
    gain_ref,
    arrived_ref,
    normed_ref,
    q_ref,
    k_ref,
    v_ref,
    stream_ref,
    advanced,
    square_out,
    square_in,
    qa,
    own,
    buf,
    m_ref,
    acc,
    recv_sem,
    sendz_sem,
    sendx_sem,
    load_sem,
    pipe_send_sem,
    pipe_recv_sem,
    square_send_sem,
    square_recv_sem,
):
    rows = q_ref.shape[0]
    pipe = lax.axis_index("pipe")
    n_pipe = lax.axis_size("pipe")
    tp = lax.axis_index("tp")
    n_tp = lax.axis_size("tp")
    following = (pipe + 1) % n_pipe
    preceding = (pipe + n_pipe - 1) % n_pipe
    ctx = lax.axis_index("ctx")
    n_ctx = lax.axis_size("ctx")
    x = ctx // NZ
    z = ctx % NZ
    right = (ctx + NZ) % n_ctx
    left = (ctx + n_ctx - NZ) % n_ctx

    barrier = pltpu.get_barrier_semaphore()
    for peer in (right, left):
        pl.semaphore_signal(barrier, inc=1, device_id={"ctx": peer}, device_id_type=MESH)

    @pl.when(z < NZ - 1)
    def _():
        pl.semaphore_signal(barrier, inc=1, device_id={"ctx": ctx + 1}, device_id_type=MESH)

    @pl.when(z > 0)
    def _():
        pl.semaphore_signal(barrier, inc=1, device_id={"ctx": ctx - 1}, device_id_type=MESH)

    for peer in (following, preceding):
        for half in range(n_tp):
            pl.semaphore_signal(
                barrier, inc=1, device_id={"pipe": peer, "tp": half}, device_id_type=MESH
            )

    loads = [
        pltpu.make_async_copy(src, dst, load_sem.at[i])
        for i, (src, dst) in enumerate(
            ((k_hbm, k_ref), (v_hbm, v_ref), (q_hbm, q_ref), (stream_hbm, stream_ref))
        )
    ]
    for load in loads:
        load.start()
    loads[0].wait()
    loads[1].wait()

    seg_f = seg_ref[...].astype(jnp.float32)
    doc_rows = lax.broadcasted_iota(jnp.int32, (OH_ROWS, rows), 0).astype(jnp.float32)
    own[0:OH_ROWS, :] = jnp.where(
        doc_rows == jnp.broadcast_to(seg_f, (OH_ROWS, rows)), 1.0, 0.0
    ).astype(jnp.bfloat16)
    for h in range(kv_heads):
        base = OH_ROWS + 2 * HEAD * h
        key_block = k_ref[:, h * HEAD : (h + 1) * HEAD].astype(jnp.float32)
        own[base : base + HEAD, :] = key_block.T.astype(jnp.bfloat16)
        own[base + HEAD : base + 2 * HEAD, :] = v_ref[:, h * HEAD : (h + 1) * HEAD]

    def part(h):
        if h == 0:
            return pl.ds(0, OH_ROWS + 2 * HEAD)
        return pl.ds(OH_ROWS + 2 * HEAD * h, 2 * HEAD)

    def copy_of(src, slot, which, h, sems, sem_row, peer):
        return pltpu.make_async_remote_copy(
            src_ref=src.at[part(h), :],
            dst_ref=buf.at[slot, which, part(h), :],
            send_sem=sems.at[sem_row, h],
            recv_sem=recv_sem.at[slot, which, h],
            device_id={"ctx": peer},
            device_id_type=MESH,
        )

    pl.semaphore_wait(barrier, 2 + 2 * n_tp + jnp.where(z < NZ - 1, 1, 0) + jnp.where(z > 0, 1, 0))

    def up(h):
        return copy_of(own, z, 0, h, sendz_sem, NZ, ctx + 1)

    def across(h):
        return copy_of(own, z, 0, h, sendx_sem, NZ, right)

    for h in range(kv_heads):
        across(h).start()

        @pl.when(z < NZ - 1)
        def _():
            up(h).start()

    loads[2].wait()
    seg_col = jnp.broadcast_to(seg_f, (rows, rows)).T
    lane = lax.broadcasted_iota(jnp.int32, (rows, HEAD), 1)
    penalty = jnp.where(
        (lane < OH_ROWS) & (lane.astype(jnp.float32) != seg_col), -FAR, 0.0
    ).astype(jnp.bfloat16)
    for h in range(kv_heads):
        for g in range(group):
            c = (h * group + g) * HEAD
            qa[h, g * rows : (g + 1) * rows, 0:HEAD] = q_ref[:, c : c + HEAD]
            qa[h, g * rows : (g + 1) * rows, HEAD : 2 * HEAD] = penalty

    scale = LOG2E * HEAD ** (-0.5)
    height = group * rows
    ones = jnp.ones((2 * rows, HEAD), jnp.bfloat16)
    pad = jnp.zeros((HEAD - OH_ROWS, 2 * rows), jnp.bfloat16)

    causal = lax.broadcasted_iota(jnp.int32, (height, rows), 0) % rows >= lax.broadcasted_iota(
        jnp.int32, (height, rows), 1
    )
    for h in range(kv_heads):
        base = OH_ROWS + 2 * HEAD * h
        rhs = jnp.concatenate(
            [own[base : base + HEAD, :], own[0:OH_ROWS, :], pad[:, 0:rows]], axis=0
        )
        s = jnp.dot(qa[h], rhs, preferred_element_type=jnp.float32)
        s = jnp.where(causal, s, -FAR)
        top = jnp.broadcast_to(jnp.max(s, axis=1, keepdims=True), (height, HEAD))
        p = jnp.exp2((s - top) * scale).astype(jnp.bfloat16)
        va = jnp.concatenate([own[base + HEAD : base + 2 * HEAD, :], ones[0:rows]], axis=1)
        m_ref[h] = top
        acc[h] = jnp.dot(p, va, preferred_element_type=jnp.float32)

    nowhere = jnp.where(
        lax.broadcasted_iota(jnp.int32, (OH_ROWS, rows), 0) == OH_ROWS - 1, 1.0, 0.0
    ).astype(jnp.bfloat16)

    def slot_of(r, k):
        return (1 - k) * (z - r) + k * (z + r - 1)

    def exists(r, k):
        return r <= (1 - k) * z + k * (NZ - z)

    def forward_z(slot, k, h):
        return copy_of(buf.at[slot, 0], slot, 0, h, sendz_sem, slot, ctx + 1 - 2 * k)

    def forward_x(slot, h):
        return copy_of(buf.at[slot, 0], slot, 1, h, sendx_sem, slot, right)

    def has_next(k):
        return (1 - k) * (NZ - 1 - z) + k * z > 0

    def relay(r):
        def one(k, carry):
            @pl.when(exists(r, k))
            def _():
                slot = slot_of(r, k)
                for h in range(kv_heads):
                    copy_of(buf.at[slot, 0], slot, 0, h, sendz_sem, slot, right).wait_recv()

                    @pl.when(has_next(k))
                    def _():
                        forward_z(slot, k, h).start()

                    forward_x(slot, h).start()

            return carry

        lax.fori_loop(0, 2, one, 0)

    def attend(r):
        def one(k, carry):
            @pl.when(exists(r, k))
            def _():
                slot = slot_of(r, k)
                for h in range(kv_heads):
                    forward_x(slot, h).wait_recv()
                known0 = x >= k
                known1 = x >= k + 1
                oh0 = jnp.where(known0, buf[slot, 0, 0:OH_ROWS, :], nowhere)
                oh1 = jnp.where(known1, buf[slot, 1, 0:OH_ROWS, :], nowhere)
                oh = jnp.concatenate([oh0, oh1], axis=1)
                for h in range(kv_heads):
                    base = OH_ROWS + 2 * HEAD * h
                    kt = jnp.concatenate(
                        [buf[slot, 0, base : base + HEAD, :], buf[slot, 1, base : base + HEAD, :]],
                        axis=1,
                    )
                    rhs = jnp.concatenate([kt, oh, pad], axis=0)
                    s = jnp.dot(qa[h], rhs, preferred_element_type=jnp.float32)
                    old = m_ref[h]
                    top = jnp.maximum(old, jnp.max(s, axis=1, keepdims=True))
                    p = jnp.exp2((s - jnp.concatenate([top, top], axis=1)) * scale)
                    fade = jnp.exp2((old - top) * scale)
                    vals = jnp.concatenate(
                        [
                            buf[slot, 0, base + HEAD : base + 2 * HEAD, :],
                            buf[slot, 1, base + HEAD : base + 2 * HEAD, :],
                        ],
                        axis=0,
                    )
                    va = jnp.concatenate([vals, ones], axis=1)
                    m_ref[h] = top
                    acc[h] = acc[h] * jnp.concatenate([fade, fade], axis=1) + jnp.dot(
                        p.astype(jnp.bfloat16), va, preferred_element_type=jnp.float32
                    )

            return carry

        lax.fori_loop(0, 2, one, 0)

    def step(r, carry):
        relay(r)

        @pl.when(r > 1)
        def _():
            attend(r - 1)

        return carry

    lax.fori_loop(1, NZ + 1, step, 0)
    attend(NZ)

    loads[3].wait()
    width = group * HEAD

    def relay_out(h):
        columns = pl.ds(h * width, width)
        return pltpu.make_async_remote_copy(
            src_ref=advanced.at[:, columns],
            dst_ref=arrived_ref.at[:, columns],
            send_sem=pipe_send_sem.at[h],
            recv_sem=pipe_recv_sem.at[h],
            device_id={"pipe": following},
            device_id_type=MESH,
        )

    squares = jnp.zeros((rows, HEAD), jnp.float32)
    for h in range(kv_heads):
        for g in range(group):
            c = (h * group + g) * HEAD
            top_rows = slice(g * rows, (g + 1) * rows)
            mixed = acc[h, top_rows, 0:HEAD] / acc[h, top_rows, HEAD : 2 * HEAD]
            mixed = mixed.astype(jnp.bfloat16).astype(jnp.float32)
            total = (stream_ref[:, c : c + HEAD].astype(jnp.float32) + mixed).astype(jnp.bfloat16)
            advanced[:, c : c + HEAD] = total
            wide = total.astype(jnp.float32)
            squares = squares + wide * wide
        relay_out(h).start()
    row_sums = jnp.broadcast_to(jnp.sum(squares, axis=1, keepdims=True), (rows, HEAD))
    square_out[...] = row_sums.T[0:8, :]

    def sums_out(t):
        return pltpu.make_async_remote_copy(
            src_ref=square_out,
            dst_ref=square_in.at[t],
            send_sem=square_send_sem.at[t],
            recv_sem=square_recv_sem.at[t],
            device_id={"pipe": following, "tp": (tp + t) % n_tp},
            device_id_type=MESH,
        )

    for t in range(n_tp):
        sums_out(n_tp - 1 - t).start()

    for h in range(kv_heads):
        across(h).wait_send()

        @pl.when(z < NZ - 1)
        def _():
            up(h).wait_send()

    def drain(r, carry):
        def one(k, inner):
            @pl.when(exists(r, k))
            def _():
                slot = slot_of(r, k)
                for h in range(kv_heads):
                    forward_x(slot, h).wait_send()

                    @pl.when(has_next(k))
                    def _():
                        forward_z(slot, k, h).wait_send()

            return inner

        lax.fori_loop(0, 2, one, 0)
        return carry

    lax.fori_loop(1, NZ + 1, drain, 0)

    for t in range(n_tp):
        sums_out(t).wait_recv()
    total = square_in[0, 0:1, :]
    for t in range(1, n_tp):
        total = total + square_in[t, 0:1, :]
    inverse = lax.rsqrt(total / (QUERY_HEADS * HEAD) + 1e-05)
    inverse = jnp.broadcast_to(inverse, (rows, rows)).T
    for h in range(kv_heads):
        relay_out(h).wait_recv()
        for g in range(group):
            c = (h * group + g) * HEAD
            wide = arrived_ref[:, c : c + HEAD].astype(jnp.float32)
            gain = gain_ref[0:1, c : c + HEAD].astype(jnp.float32)
            normed_ref[:, c : c + HEAD] = (wide * inverse * gain).astype(jnp.bfloat16)
    for h in range(kv_heads):
        relay_out(h).wait_send()
    for t in range(n_tp):
        sums_out(t).wait_send()


def per_device(stream, queries, keys, values, segments, norm_gain):
    stream, queries, keys, values = stream[0], queries[0], keys[0], values[0]
    rows = queries.shape[0]
    kv_heads = keys.shape[1] // HEAD
    group = queries.shape[1] // keys.shape[1]
    block_rows = OH_ROWS + 2 * HEAD * kv_heads
    n_tp = lax.axis_size("tp")
    vmem = pl.BlockSpec(memory_space=pltpu.VMEM)
    anywhere = pl.BlockSpec(memory_space=pltpu.HBM)
    like_stream = jax.ShapeDtypeStruct(stream.shape, jnp.bfloat16)
    arrived, normed = pl.pallas_call(
        functools.partial(attention_kernel, kv_heads, group),
        out_shape=(like_stream, like_stream),
        in_specs=[anywhere] * 4 + [vmem] * 2,
        out_specs=(vmem, vmem),
        scratch_shapes=[
            pltpu.VMEM(queries.shape, jnp.bfloat16),
            pltpu.VMEM(keys.shape, jnp.bfloat16),
            pltpu.VMEM(values.shape, jnp.bfloat16),
            pltpu.VMEM(stream.shape, jnp.bfloat16),
            pltpu.VMEM(stream.shape, jnp.bfloat16),
            pltpu.VMEM((8, rows), jnp.float32),
            pltpu.VMEM((n_tp, 8, rows), jnp.float32),
            pltpu.VMEM((kv_heads, group * rows, 2 * HEAD), jnp.bfloat16),
            pltpu.VMEM((block_rows, rows), jnp.bfloat16),
            pltpu.VMEM((NZ, 2, block_rows, rows), jnp.bfloat16),
            pltpu.VMEM((kv_heads, group * rows, HEAD), jnp.float32),
            pltpu.VMEM((kv_heads, group * rows, 2 * HEAD), jnp.float32),
            pltpu.SemaphoreType.DMA((NZ, 2, kv_heads)),
            pltpu.SemaphoreType.DMA((NZ + 1, kv_heads)),
            pltpu.SemaphoreType.DMA((NZ + 1, kv_heads)),
            pltpu.SemaphoreType.DMA((4,)),
            pltpu.SemaphoreType.DMA((kv_heads,)),
            pltpu.SemaphoreType.DMA((kv_heads,)),
            pltpu.SemaphoreType.DMA((n_tp,)),
            pltpu.SemaphoreType.DMA((n_tp,)),
        ],
        compiler_params=pltpu.CompilerParams(
            collective_id=0, has_side_effects=True, vmem_limit_bytes=48 * 1024 * 1024
        ),
    )(queries, keys, values, stream, segments, norm_gain[None])
    return (arrived[None], normed[None])


def solution(mesh):
    in_specs = (
        P("pipe", "ctx", "tp"),
        P("pipe", "ctx", "tp"),
        P("pipe", "ctx", "tp"),
        P("pipe", "ctx", "tp"),
        P("pipe", "ctx"),
        P("tp"),
    )
    out_specs = (P("pipe", "ctx", "tp"), P("pipe", "ctx", "tp"))
    return jax.shard_map(
        per_device, mesh=mesh, in_specs=in_specs, out_specs=out_specs, check_vma=False
    )
```

```python
import functools

import jax
import jax.numpy as jnp
from jax import lax
from jax.experimental import pallas as pl
from jax.experimental.pallas import tpu as pltpu
from jax.sharding import PartitionSpec as P

QUERY_HEADS = 32
HEAD = 128
MESH = pl.DeviceIdType.MESH
NZ = 8
OH_ROWS = 16
FAR = float(2**20)
LOG2E = 1.4426950408889634


def attention_kernel(
    kv_heads,
    group,
    q_hbm,
    k_hbm,
    v_hbm,
    stream_hbm,
    seg_hbm,
    gain_hbm,
    arrived_ref,
    normed_ref,
    q_ref,
    k_ref,
    v_ref,
    stream_ref,
    seg_ref,
    gain_ref,
    advanced,
    square_out,
    square_in,
    qa,
    own,
    passing,
    buf,
    m_ref,
    acc,
    recv_sem,
    sendz_sem,
    sendx_sem,
    pass_recv_sem,
    pass_send_sem,
    load_sem,
    pipe_send_sem,
    pipe_recv_sem,
    square_send_sem,
    square_recv_sem,
):
    rows = q_ref.shape[0]
    pipe = lax.axis_index("pipe")
    n_pipe = lax.axis_size("pipe")
    tp = lax.axis_index("tp")
    n_tp = lax.axis_size("tp")
    following = (pipe + 1) % n_pipe
    preceding = (pipe + n_pipe - 1) % n_pipe
    ctx = lax.axis_index("ctx")
    n_ctx = lax.axis_size("ctx")
    x = ctx // NZ
    z = ctx % NZ
    right = (ctx + NZ) % n_ctx
    left = (ctx + n_ctx - NZ) % n_ctx

    loads = [
        pltpu.make_async_copy(src, dst, load_sem.at[i])
        for i, (src, dst) in enumerate(
            (
                (seg_hbm, seg_ref),
                (k_hbm, k_ref),
                (v_hbm, v_ref),
                (q_hbm, q_ref),
                (stream_hbm, stream_ref),
                (gain_hbm, gain_ref),
            )
        )
    ]
    for load in loads:
        load.start()

    barrier = pltpu.get_barrier_semaphore()
    for peer in (right, left):
        pl.semaphore_signal(barrier, inc=1, device_id={"ctx": peer}, device_id_type=MESH)

    @pl.when(z < NZ - 1)
    def _():
        pl.semaphore_signal(barrier, inc=1, device_id={"ctx": ctx + 1}, device_id_type=MESH)

    @pl.when(z > 0)
    def _():
        pl.semaphore_signal(barrier, inc=1, device_id={"ctx": ctx - 1}, device_id_type=MESH)

    for peer in (following, preceding):
        for half in range(n_tp):
            pl.semaphore_signal(
                barrier, inc=1, device_id={"pipe": peer, "tp": half}, device_id_type=MESH
            )

    def part(h):
        if h == 0:
            return pl.ds(0, OH_ROWS + 2 * HEAD)
        return pl.ds(OH_ROWS + 2 * HEAD * h, 2 * HEAD)

    def send(src, dst, h, send_sem, arrive_sem, peer):
        return pltpu.make_async_remote_copy(
            src_ref=src.at[part(h), :],
            dst_ref=dst.at[part(h), :],
            send_sem=send_sem,
            recv_sem=arrive_sem,
            device_id={"ctx": peer},
            device_id_type=MESH,
        )

    def copy_of(src, slot, which, h, send_sem, peer):
        return send(src, buf.at[slot, which], h, send_sem, recv_sem.at[slot, which, h], peer)

    def up(h):
        return copy_of(own, z, 0, h, sendz_sem.at[NZ, h], ctx + 1)

    def across(h):
        return copy_of(own, z, 0, h, sendx_sem.at[NZ, h], right)

    def pass_first(h):
        return send(own, passing, h, pass_send_sem.at[0, h], pass_recv_sem.at[h], left)

    def pass_second(h):
        return copy_of(passing, z, 1, h, pass_send_sem.at[1, h], left)

    for load in loads[:3]:
        load.wait()
    seg_f = seg_ref[...].astype(jnp.float32)
    doc_rows = lax.broadcasted_iota(jnp.int32, (OH_ROWS, rows), 0).astype(jnp.float32)
    own[0:OH_ROWS, :] = jnp.where(
        doc_rows == jnp.broadcast_to(seg_f, (OH_ROWS, rows)), 1.0, 0.0
    ).astype(jnp.bfloat16)
    for h in range(kv_heads):
        base = OH_ROWS + 2 * HEAD * h
        key_block = k_ref[:, h * HEAD : (h + 1) * HEAD].astype(jnp.float32)
        own[base : base + HEAD, :] = key_block.T.astype(jnp.bfloat16)
        own[base + HEAD : base + 2 * HEAD, :] = v_ref[:, h * HEAD : (h + 1) * HEAD]
        if h == 0:
            pl.semaphore_wait(
                barrier,
                2 + 2 * n_tp + jnp.where(z < NZ - 1, 1, 0) + jnp.where(z > 0, 1, 0),
            )
        across(h).start()

        @pl.when(z < NZ - 1)
        def _():
            up(h).start()

        pass_first(h).start()

    loads[3].wait()
    seg_col = jnp.broadcast_to(seg_f, (rows, rows)).T
    lane = lax.broadcasted_iota(jnp.int32, (rows, HEAD), 1)
    penalty = jnp.where(
        (lane < OH_ROWS) & (lane.astype(jnp.float32) != seg_col), -FAR, 0.0
    ).astype(jnp.bfloat16)
    for h in range(kv_heads):
        for g in range(group):
            c = (h * group + g) * HEAD
            qa[h, g * rows : (g + 1) * rows, 0:HEAD] = q_ref[:, c : c + HEAD]
            qa[h, g * rows : (g + 1) * rows, HEAD : 2 * HEAD] = penalty

    scale = LOG2E * HEAD ** (-0.5)
    height = group * rows
    ones = jnp.ones((2 * rows, HEAD), jnp.bfloat16)
    pad = jnp.zeros((HEAD - OH_ROWS, 2 * rows), jnp.bfloat16)

    causal = lax.broadcasted_iota(jnp.int32, (height, rows), 0) % rows >= lax.broadcasted_iota(
        jnp.int32, (height, rows), 1
    )

    def attend_own(h):
        base = OH_ROWS + 2 * HEAD * h
        rhs = jnp.concatenate(
            [own[base : base + HEAD, :], own[0:OH_ROWS, :], pad[:, 0:rows]], axis=0
        )
        s = jnp.dot(qa[h], rhs, preferred_element_type=jnp.float32)
        s = jnp.where(causal, s, -FAR)
        top = jnp.broadcast_to(jnp.max(s, axis=1, keepdims=True), (height, HEAD))
        p = jnp.exp2((s - top) * scale).astype(jnp.bfloat16)
        va = jnp.concatenate([own[base + HEAD : base + 2 * HEAD, :], ones[0:rows]], axis=1)
        m_ref[h] = top
        acc[h] = jnp.dot(p, va, preferred_element_type=jnp.float32)

    nowhere = jnp.where(
        lax.broadcasted_iota(jnp.int32, (OH_ROWS, rows), 0) == OH_ROWS - 1, 1.0, 0.0
    ).astype(jnp.bfloat16)

    both = jnp.minimum(z, NZ - z)

    def place(t):
        paired = jnp.where(t <= 2 * both, 1, 0)
        r = paired * ((t + 1) // 2) + (1 - paired) * (t - both)
        tall = jnp.where(z > NZ - z, 0, 1)
        k = paired * ((t + 1) % 2) + (1 - paired) * tall
        slot = (1 - k) * (z - r) + k * (z + r - 1)
        onward = (1 - k) * (NZ - 1 - z) + k * z > 0
        first_of_beyond = r + NZ * (1 - k) == 1
        return slot, k, onward, first_of_beyond

    def forward_z(slot, k, h):
        return copy_of(buf.at[slot, 0], slot, 0, h, sendz_sem.at[slot, h], ctx + 1 - 2 * k)

    def forward_x(slot, h):
        return copy_of(buf.at[slot, 0], slot, 1, h, sendx_sem.at[slot, h], right)

    def relay(at, h):
        slot, k, onward, first_of_beyond = at
        across_wait = copy_of(buf.at[slot, 0], slot, 0, h, sendz_sem.at[slot, h], right)
        across_wait.wait_recv()

        @pl.when(onward)
        def _():
            forward_z(slot, k, h).start()

        @pl.when(jnp.logical_not(first_of_beyond))
        def _():
            forward_x(slot, h).start()

    def attend(at, h):
        slot, k, _, _ = at
        forward_x(slot, h).wait_recv()
        oh0 = jnp.where(x >= k, buf[slot, 0, 0:OH_ROWS, :], nowhere)
        oh1 = jnp.where(x >= k + 1, buf[slot, 1, 0:OH_ROWS, :], nowhere)
        oh = jnp.concatenate([oh0, oh1], axis=1)
        base = OH_ROWS + 2 * HEAD * h
        kt = jnp.concatenate(
            [buf[slot, 0, base : base + HEAD, :], buf[slot, 1, base : base + HEAD, :]],
            axis=1,
        )
        rhs = jnp.concatenate([kt, oh, pad], axis=0)
        s = jnp.dot(qa[h], rhs, preferred_element_type=jnp.float32)
        old = m_ref[h]
        top = jnp.maximum(old, jnp.max(s, axis=1, keepdims=True))
        p = jnp.exp2((s - jnp.concatenate([top, top], axis=1)) * scale)
        fade = jnp.exp2((old - top) * scale)
        vals = jnp.concatenate(
            [
                buf[slot, 0, base + HEAD : base + 2 * HEAD, :],
                buf[slot, 1, base + HEAD : base + 2 * HEAD, :],
            ],
            axis=0,
        )
        va = jnp.concatenate([vals, ones], axis=1)
        m_ref[h] = top
        acc[h] = acc[h] * jnp.concatenate([fade, fade], axis=1) + jnp.dot(
            p.astype(jnp.bfloat16), va, preferred_element_type=jnp.float32
        )

    first = place(1)
    for h in range(kv_heads):
        pass_first(h).wait_recv()
        pass_second(h).start()
        relay(first, h)
        attend_own(h)

    def step(t, carry):
        now, before = place(t), place(t - 1)
        for h in range(kv_heads):
            relay(now, h)
            attend(before, h)
        return carry

    lax.fori_loop(2, NZ + 1, step, 0)

    loads[4].wait()
    loads[5].wait()
    width = group * HEAD

    def relay_out(h):
        columns = pl.ds(h * width, width)
        return pltpu.make_async_remote_copy(
            src_ref=advanced.at[:, columns],
            dst_ref=arrived_ref.at[:, columns],
            send_sem=pipe_send_sem.at[h],
            recv_sem=pipe_recv_sem.at[h],
            device_id={"pipe": following},
            device_id_type=MESH,
        )

    last = place(NZ)
    squares = jnp.zeros((rows, HEAD), jnp.float32)
    for h in range(kv_heads):
        attend(last, h)
        for g in range(group):
            c = (h * group + g) * HEAD
            top_rows = slice(g * rows, (g + 1) * rows)
            mixed = acc[h, top_rows, 0:HEAD] / acc[h, top_rows, HEAD : 2 * HEAD]
            mixed = mixed.astype(jnp.bfloat16).astype(jnp.float32)
            total = (stream_ref[:, c : c + HEAD].astype(jnp.float32) + mixed).astype(jnp.bfloat16)
            advanced[:, c : c + HEAD] = total
            wide = total.astype(jnp.float32)
            squares = squares + wide * wide
        relay_out(h).start()
    row_sums = jnp.broadcast_to(jnp.sum(squares, axis=1, keepdims=True), (rows, HEAD))
    square_out[...] = row_sums.T[0:8, :]

    def sums_out(t):
        return pltpu.make_async_remote_copy(
            src_ref=square_out,
            dst_ref=square_in.at[t],
            send_sem=square_send_sem.at[t],
            recv_sem=square_recv_sem.at[t],
            device_id={"pipe": following, "tp": (tp + t) % n_tp},
            device_id_type=MESH,
        )

    for t in range(n_tp):
        sums_out(n_tp - 1 - t).start()

    for h in range(kv_heads):
        across(h).wait_send()
        pass_first(h).wait_send()
        pass_second(h).wait_send()

        @pl.when(z < NZ - 1)
        def _():
            up(h).wait_send()

    def drain(t, carry):
        slot, k, onward, first_of_beyond = place(t)
        for h in range(kv_heads):

            @pl.when(onward)
            def _():
                forward_z(slot, k, h).wait_send()

            @pl.when(jnp.logical_not(first_of_beyond))
            def _():
                forward_x(slot, h).wait_send()

        return carry

    lax.fori_loop(1, NZ + 1, drain, 0)

    for t in range(n_tp):
        sums_out(t).wait_recv()
    total = square_in[0, 0:1, :]
    for t in range(1, n_tp):
        total = total + square_in[t, 0:1, :]
    inverse = lax.rsqrt(total / (QUERY_HEADS * HEAD) + 1e-05)
    inverse = jnp.broadcast_to(inverse, (rows, rows)).T
    for h in range(kv_heads):
        relay_out(h).wait_recv()
        for g in range(group):
            c = (h * group + g) * HEAD
            wide = arrived_ref[:, c : c + HEAD].astype(jnp.float32)
            gain = gain_ref[c : c + HEAD].astype(jnp.float32)[None, :]
            normed_ref[:, c : c + HEAD] = (wide * inverse * gain).astype(jnp.bfloat16)
    for h in range(kv_heads):
        relay_out(h).wait_send()
    for t in range(n_tp):
        sums_out(t).wait_send()


def per_device(stream, queries, keys, values, segments, norm_gain):
    stream, queries, keys, values = stream[0], queries[0], keys[0], values[0]
    rows = queries.shape[0]
    kv_heads = keys.shape[1] // HEAD
    group = queries.shape[1] // keys.shape[1]
    block_rows = OH_ROWS + 2 * HEAD * kv_heads
    n_tp = lax.axis_size("tp")
    vmem = pl.BlockSpec(memory_space=pltpu.VMEM)
    anywhere = pl.BlockSpec(memory_space=pltpu.HBM)
    like_stream = jax.ShapeDtypeStruct(stream.shape, jnp.bfloat16)
    arrived, normed = pl.pallas_call(
        functools.partial(attention_kernel, kv_heads, group),
        out_shape=(like_stream, like_stream),
        in_specs=[anywhere] * 6,
        out_specs=(vmem, vmem),
        scratch_shapes=[
            pltpu.VMEM(queries.shape, jnp.bfloat16),
            pltpu.VMEM(keys.shape, jnp.bfloat16),
            pltpu.VMEM(values.shape, jnp.bfloat16),
            pltpu.VMEM(stream.shape, jnp.bfloat16),
            pltpu.VMEM(segments.shape, segments.dtype),
            pltpu.VMEM(norm_gain.shape, jnp.bfloat16),
            pltpu.VMEM(stream.shape, jnp.bfloat16),
            pltpu.VMEM((8, rows), jnp.float32),
            pltpu.VMEM((n_tp, 8, rows), jnp.float32),
            pltpu.VMEM((kv_heads, group * rows, 2 * HEAD), jnp.bfloat16),
            pltpu.VMEM((block_rows, rows), jnp.bfloat16),
            pltpu.VMEM((block_rows, rows), jnp.bfloat16),
            pltpu.VMEM((NZ, 2, block_rows, rows), jnp.bfloat16),
            pltpu.VMEM((kv_heads, group * rows, HEAD), jnp.float32),
            pltpu.VMEM((kv_heads, group * rows, 2 * HEAD), jnp.float32),
            pltpu.SemaphoreType.DMA((NZ, 2, kv_heads)),
            pltpu.SemaphoreType.DMA((NZ + 1, kv_heads)),
            pltpu.SemaphoreType.DMA((NZ + 1, kv_heads)),
            pltpu.SemaphoreType.DMA((kv_heads,)),
            pltpu.SemaphoreType.DMA((2, kv_heads)),
            pltpu.SemaphoreType.DMA((6,)),
            pltpu.SemaphoreType.DMA((kv_heads,)),
            pltpu.SemaphoreType.DMA((kv_heads,)),
            pltpu.SemaphoreType.DMA((n_tp,)),
            pltpu.SemaphoreType.DMA((n_tp,)),
        ],
        compiler_params=pltpu.CompilerParams(
            collective_id=0, has_side_effects=True, vmem_limit_bytes=63 * 1024 * 1024
        ),
    )(queries, keys, values, stream, segments, norm_gain)
    return (arrived[None], normed[None])


def solution(mesh):
    in_specs = (
        P("pipe", "ctx", "tp"),
        P("pipe", "ctx", "tp"),
        P("pipe", "ctx", "tp"),
        P("pipe", "ctx", "tp"),
        P("pipe", "ctx"),
        P("tp"),
    )
    out_specs = (P("pipe", "ctx", "tp"), P("pipe", "ctx", "tp"))
    return jax.shard_map(
        per_device, mesh=mesh, in_specs=in_specs, out_specs=out_specs, check_vma=False
    )
```

```python
import functools

import jax
import jax.numpy as jnp
from jax import lax
from jax.experimental import pallas as pl
from jax.experimental.pallas import tpu as pltpu
from jax.sharding import PartitionSpec as P

QUERY_HEADS = 32
HEAD = 128
MESH = pl.DeviceIdType.MESH
NZ = 8
OH_ROWS = 16
LAG = 3
FAR = float(2**20)
LOG2E = 1.4426950408889634


def attention_kernel(
    kv_heads,
    group,
    q_hbm,
    k_hbm,
    v_hbm,
    stream_hbm,
    seg_hbm,
    gain_hbm,
    arrived_ref,
    normed_ref,
    q_ref,
    k_ref,
    v_ref,
    stream_ref,
    seg_ref,
    gain_ref,
    advanced,
    square_out,
    square_in,
    qa,
    own,
    passing,
    buf,
    m_ref,
    acc,
    recv_sem,
    sendz_sem,
    sendx_sem,
    pass_recv_sem,
    pass_send_sem,
    load_sem,
    pipe_send_sem,
    pipe_recv_sem,
    square_send_sem,
    square_recv_sem,
):
    rows = q_ref.shape[0]
    pipe = lax.axis_index("pipe")
    n_pipe = lax.axis_size("pipe")
    tp = lax.axis_index("tp")
    n_tp = lax.axis_size("tp")
    following = (pipe + 1) % n_pipe
    preceding = (pipe + n_pipe - 1) % n_pipe
    ctx = lax.axis_index("ctx")
    n_ctx = lax.axis_size("ctx")
    x = ctx // NZ
    z = ctx % NZ
    right = (ctx + NZ) % n_ctx
    left = (ctx + n_ctx - NZ) % n_ctx

    loads = [
        pltpu.make_async_copy(src, dst, load_sem.at[i])
        for i, (src, dst) in enumerate(
            (
                (seg_hbm, seg_ref),
                (k_hbm, k_ref),
                (v_hbm, v_ref),
                (q_hbm, q_ref),
                (stream_hbm, stream_ref),
                (gain_hbm, gain_ref),
            )
        )
    ]
    for load in loads:
        load.start()

    barrier = pltpu.get_barrier_semaphore()
    for peer in (right, left):
        pl.semaphore_signal(barrier, inc=1, device_id={"ctx": peer}, device_id_type=MESH)

    @pl.when(z < NZ - 1)
    def _():
        pl.semaphore_signal(barrier, inc=1, device_id={"ctx": ctx + 1}, device_id_type=MESH)

    @pl.when(z > 0)
    def _():
        pl.semaphore_signal(barrier, inc=1, device_id={"ctx": ctx - 1}, device_id_type=MESH)

    for peer in (following, preceding):
        for half in range(n_tp):
            pl.semaphore_signal(
                barrier, inc=1, device_id={"pipe": peer, "tp": half}, device_id_type=MESH
            )

    def part(h):
        if h == 0:
            return pl.ds(0, OH_ROWS + 2 * HEAD)
        return pl.ds(OH_ROWS + 2 * HEAD * h, 2 * HEAD)

    def send(src, dst, h, send_sem, arrive_sem, peer):
        return pltpu.make_async_remote_copy(
            src_ref=src.at[part(h), :],
            dst_ref=dst.at[part(h), :],
            send_sem=send_sem,
            recv_sem=arrive_sem,
            device_id={"ctx": peer},
            device_id_type=MESH,
        )

    def copy_of(src, slot, which, h, send_sem, peer):
        return send(src, buf.at[slot, which], h, send_sem, recv_sem.at[slot, which, h], peer)

    def up(h):
        return copy_of(own, z, 0, h, sendz_sem.at[NZ, h], ctx + 1)

    def across(h):
        return copy_of(own, z, 0, h, sendx_sem.at[NZ, h], right)

    def pass_first(h):
        return send(own, passing, h, pass_send_sem.at[0, h], pass_recv_sem.at[h], left)

    def pass_second(h):
        return copy_of(passing, z, 1, h, pass_send_sem.at[1, h], left)

    for load in loads[:3]:
        load.wait()
    seg_f = seg_ref[...].astype(jnp.float32)
    doc_rows = lax.broadcasted_iota(jnp.int32, (OH_ROWS, rows), 0).astype(jnp.float32)
    own[0:OH_ROWS, :] = jnp.where(
        doc_rows == jnp.broadcast_to(seg_f, (OH_ROWS, rows)), 1.0, 0.0
    ).astype(jnp.bfloat16)
    for h in range(kv_heads):
        base = OH_ROWS + 2 * HEAD * h
        key_block = k_ref[:, h * HEAD : (h + 1) * HEAD].astype(jnp.float32)
        own[base : base + HEAD, :] = key_block.T.astype(jnp.bfloat16)
        own[base + HEAD : base + 2 * HEAD, :] = v_ref[:, h * HEAD : (h + 1) * HEAD]
        if h == 0:
            pl.semaphore_wait(
                barrier,
                2 + 2 * n_tp + jnp.where(z < NZ - 1, 1, 0) + jnp.where(z > 0, 1, 0),
            )
        across(h).start()

        @pl.when(z < NZ - 1)
        def _():
            up(h).start()

        pass_first(h).start()

    loads[3].wait()
    seg_col = jnp.broadcast_to(seg_f, (rows, rows)).T
    lane = lax.broadcasted_iota(jnp.int32, (rows, HEAD), 1)
    penalty = jnp.where(
        (lane < OH_ROWS) & (lane.astype(jnp.float32) != seg_col), -FAR, 0.0
    ).astype(jnp.bfloat16)
    for h in range(kv_heads):
        for g in range(group):
            c = (h * group + g) * HEAD
            qa[h, g * rows : (g + 1) * rows, 0:HEAD] = q_ref[:, c : c + HEAD]
            qa[h, g * rows : (g + 1) * rows, HEAD : 2 * HEAD] = penalty

    scale = LOG2E * HEAD ** (-0.5)
    height = group * rows
    ones = jnp.ones((2 * rows, HEAD), jnp.bfloat16)
    pad = jnp.zeros((HEAD - OH_ROWS, 2 * rows), jnp.bfloat16)

    causal = lax.broadcasted_iota(jnp.int32, (height, rows), 0) % rows >= lax.broadcasted_iota(
        jnp.int32, (height, rows), 1
    )

    def attend_own(h):
        base = OH_ROWS + 2 * HEAD * h
        rhs = jnp.concatenate(
            [own[base : base + HEAD, :], own[0:OH_ROWS, :], pad[:, 0:rows]], axis=0
        )
        s = jnp.dot(qa[h], rhs, preferred_element_type=jnp.float32)
        s = jnp.where(causal, s, -FAR)
        top = jnp.broadcast_to(jnp.max(s, axis=1, keepdims=True), (height, HEAD))
        p = jnp.exp2((s - top) * scale).astype(jnp.bfloat16)
        va = jnp.concatenate([own[base + HEAD : base + 2 * HEAD, :], ones[0:rows]], axis=1)
        m_ref[h] = top
        acc[h] = jnp.dot(p, va, preferred_element_type=jnp.float32)

    nowhere = jnp.where(
        lax.broadcasted_iota(jnp.int32, (OH_ROWS, rows), 0) == OH_ROWS - 1, 1.0, 0.0
    ).astype(jnp.bfloat16)

    both = jnp.minimum(z, NZ - z)

    def place(t):
        paired = jnp.where(t <= 2 * both, 1, 0)
        r = paired * ((t + 1) // 2) + (1 - paired) * (t - both)
        tall = jnp.where(z > NZ - z, 0, 1)
        k = paired * (t % 2) + (1 - paired) * tall
        slot = (1 - k) * (z - r) + k * (z + r - 1)
        onward = (1 - k) * (NZ - 1 - z) + k * z > 0
        first_of_beyond = r + NZ * (1 - k) == 1
        return slot, k, onward, first_of_beyond

    def forward_z(slot, k, h):
        return copy_of(buf.at[slot, 0], slot, 0, h, sendz_sem.at[slot, h], ctx + 1 - 2 * k)

    def forward_x(slot, h):
        return copy_of(buf.at[slot, 0], slot, 1, h, sendx_sem.at[slot, h], right)

    def relay(at, h):
        slot, k, onward, first_of_beyond = at
        across_wait = copy_of(buf.at[slot, 0], slot, 0, h, sendz_sem.at[slot, h], right)
        across_wait.wait_recv()

        @pl.when(onward)
        def _():
            forward_z(slot, k, h).start()

        @pl.when(jnp.logical_not(first_of_beyond))
        def _():
            forward_x(slot, h).start()

    def attend(at, h):
        slot, k, _, _ = at
        forward_x(slot, h).wait_recv()
        oh0 = jnp.where(x >= k, buf[slot, 0, 0:OH_ROWS, :], nowhere)
        oh1 = jnp.where(x >= k + 1, buf[slot, 1, 0:OH_ROWS, :], nowhere)
        oh = jnp.concatenate([oh0, oh1], axis=1)
        base = OH_ROWS + 2 * HEAD * h
        kt = jnp.concatenate(
            [buf[slot, 0, base : base + HEAD, :], buf[slot, 1, base : base + HEAD, :]],
            axis=1,
        )
        rhs = jnp.concatenate([kt, oh, pad], axis=0)
        s = jnp.dot(qa[h], rhs, preferred_element_type=jnp.float32)
        old = m_ref[h]
        top = jnp.maximum(old, jnp.max(s, axis=1, keepdims=True))
        p = jnp.exp2((s - jnp.concatenate([top, top], axis=1)) * scale)
        fade = jnp.exp2((old - top) * scale)
        vals = jnp.concatenate(
            [
                buf[slot, 0, base + HEAD : base + 2 * HEAD, :],
                buf[slot, 1, base + HEAD : base + 2 * HEAD, :],
            ],
            axis=0,
        )
        va = jnp.concatenate([vals, ones], axis=1)
        m_ref[h] = top
        acc[h] = acc[h] * jnp.concatenate([fade, fade], axis=1) + jnp.dot(
            p.astype(jnp.bfloat16), va, preferred_element_type=jnp.float32
        )

    first = place(1)
    for h in range(kv_heads):
        pass_first(h).wait_recv()
        pass_second(h).start()
        relay(first, h)
        attend_own(h)

    def step(t, carry):
        now, before = place(t), place(t - LAG)
        for h in range(kv_heads):
            relay(now, h)
            attend(before, h)
        return carry

    def step_without(t, carry):
        now = place(t)
        for h in range(kv_heads):
            relay(now, h)
        return carry

    lax.fori_loop(2, LAG + 1, step_without, 0)
    lax.fori_loop(LAG + 1, NZ + 1, step, 0)

    loads[4].wait()
    loads[5].wait()
    width = group * HEAD

    def relay_out(h):
        columns = pl.ds(h * width, width)
        return pltpu.make_async_remote_copy(
            src_ref=advanced.at[:, columns],
            dst_ref=arrived_ref.at[:, columns],
            send_sem=pipe_send_sem.at[h],
            recv_sem=pipe_recv_sem.at[h],
            device_id={"pipe": following},
            device_id_type=MESH,
        )

    squares = jnp.zeros((rows, HEAD), jnp.float32)
    for h in range(kv_heads):

        def rest(t, carry):
            attend(place(t), h)
            return carry

        lax.fori_loop(NZ - LAG + 1, NZ + 1, rest, 0)
        for g in range(group):
            c = (h * group + g) * HEAD
            top_rows = slice(g * rows, (g + 1) * rows)
            mixed = acc[h, top_rows, 0:HEAD] / acc[h, top_rows, HEAD : 2 * HEAD]
            mixed = mixed.astype(jnp.bfloat16).astype(jnp.float32)
            total = (stream_ref[:, c : c + HEAD].astype(jnp.float32) + mixed).astype(jnp.bfloat16)
            advanced[:, c : c + HEAD] = total
            wide = total.astype(jnp.float32)
            squares = squares + wide * wide
        relay_out(h).start()
    row_sums = jnp.broadcast_to(jnp.sum(squares, axis=1, keepdims=True), (rows, HEAD))
    square_out[...] = row_sums.T[0:8, :]

    def sums_out(t):
        return pltpu.make_async_remote_copy(
            src_ref=square_out,
            dst_ref=square_in.at[t],
            send_sem=square_send_sem.at[t],
            recv_sem=square_recv_sem.at[t],
            device_id={"pipe": following, "tp": (tp + t) % n_tp},
            device_id_type=MESH,
        )

    for t in range(n_tp):
        sums_out(n_tp - 1 - t).start()

    for h in range(kv_heads):
        across(h).wait_send()
        pass_first(h).wait_send()
        pass_second(h).wait_send()

        @pl.when(z < NZ - 1)
        def _():
            up(h).wait_send()

    def drain(t, carry):
        slot, k, onward, first_of_beyond = place(t)
        for h in range(kv_heads):

            @pl.when(onward)
            def _():
                forward_z(slot, k, h).wait_send()

            @pl.when(jnp.logical_not(first_of_beyond))
            def _():
                forward_x(slot, h).wait_send()

        return carry

    lax.fori_loop(1, NZ + 1, drain, 0)

    for t in range(n_tp):
        sums_out(t).wait_recv()
    total = square_in[0, 0:1, :]
    for t in range(1, n_tp):
        total = total + square_in[t, 0:1, :]
    inverse = lax.rsqrt(total / (QUERY_HEADS * HEAD) + 1e-05)
    inverse = jnp.broadcast_to(inverse, (rows, rows)).T
    for h in range(kv_heads):
        relay_out(h).wait_recv()
        for g in range(group):
            c = (h * group + g) * HEAD
            wide = arrived_ref[:, c : c + HEAD].astype(jnp.float32)
            gain = gain_ref[c : c + HEAD].astype(jnp.float32)[None, :]
            normed_ref[:, c : c + HEAD] = (wide * inverse * gain).astype(jnp.bfloat16)
    for h in range(kv_heads):
        relay_out(h).wait_send()
    for t in range(n_tp):
        sums_out(t).wait_send()


def per_device(stream, queries, keys, values, segments, norm_gain):
    stream, queries, keys, values = stream[0], queries[0], keys[0], values[0]
    rows = queries.shape[0]
    kv_heads = keys.shape[1] // HEAD
    group = queries.shape[1] // keys.shape[1]
    block_rows = OH_ROWS + 2 * HEAD * kv_heads
    n_tp = lax.axis_size("tp")
    vmem = pl.BlockSpec(memory_space=pltpu.VMEM)
    anywhere = pl.BlockSpec(memory_space=pltpu.HBM)
    like_stream = jax.ShapeDtypeStruct(stream.shape, jnp.bfloat16)
    arrived, normed = pl.pallas_call(
        functools.partial(attention_kernel, kv_heads, group),
        out_shape=(like_stream, like_stream),
        in_specs=[anywhere] * 6,
        out_specs=(vmem, vmem),
        scratch_shapes=[
            pltpu.VMEM(queries.shape, jnp.bfloat16),
            pltpu.VMEM(keys.shape, jnp.bfloat16),
            pltpu.VMEM(values.shape, jnp.bfloat16),
            pltpu.VMEM(stream.shape, jnp.bfloat16),
            pltpu.VMEM(segments.shape, segments.dtype),
            pltpu.VMEM(norm_gain.shape, jnp.bfloat16),
            pltpu.VMEM(stream.shape, jnp.bfloat16),
            pltpu.VMEM((8, rows), jnp.float32),
            pltpu.VMEM((n_tp, 8, rows), jnp.float32),
            pltpu.VMEM((kv_heads, group * rows, 2 * HEAD), jnp.bfloat16),
            pltpu.VMEM((block_rows, rows), jnp.bfloat16),
            pltpu.VMEM((block_rows, rows), jnp.bfloat16),
            pltpu.VMEM((NZ, 2, block_rows, rows), jnp.bfloat16),
            pltpu.VMEM((kv_heads, group * rows, HEAD), jnp.float32),
            pltpu.VMEM((kv_heads, group * rows, 2 * HEAD), jnp.float32),
            pltpu.SemaphoreType.DMA((NZ, 2, kv_heads)),
            pltpu.SemaphoreType.DMA((NZ + 1, kv_heads)),
            pltpu.SemaphoreType.DMA((NZ + 1, kv_heads)),
            pltpu.SemaphoreType.DMA((kv_heads,)),
            pltpu.SemaphoreType.DMA((2, kv_heads)),
            pltpu.SemaphoreType.DMA((6,)),
            pltpu.SemaphoreType.DMA((kv_heads,)),
            pltpu.SemaphoreType.DMA((kv_heads,)),
            pltpu.SemaphoreType.DMA((n_tp,)),
            pltpu.SemaphoreType.DMA((n_tp,)),
        ],
        compiler_params=pltpu.CompilerParams(
            collective_id=0, has_side_effects=True, vmem_limit_bytes=63 * 1024 * 1024
        ),
    )(queries, keys, values, stream, segments, norm_gain)
    return (arrived[None], normed[None])


def solution(mesh):
    in_specs = (
        P("pipe", "ctx", "tp"),
        P("pipe", "ctx", "tp"),
        P("pipe", "ctx", "tp"),
        P("pipe", "ctx", "tp"),
        P("pipe", "ctx"),
        P("tp"),
    )
    out_specs = (P("pipe", "ctx", "tp"), P("pipe", "ctx", "tp"))
    return jax.shard_map(
        per_device, mesh=mesh, in_specs=in_specs, out_specs=out_specs, check_vma=False
    )
```

```python
import functools

import jax
import jax.numpy as jnp
from jax import lax
from jax.experimental import pallas as pl
from jax.experimental.pallas import tpu as pltpu
from jax.sharding import PartitionSpec as P

QUERY_HEADS = 32
HEAD = 128
MESH = pl.DeviceIdType.MESH
NZ = 8
OH_ROWS = 16
NORM_COLUMNS = 1024
LAG = 3
FAR = float(2**20)
LOG2E = 1.4426950408889634


def attention_kernel(
    kv_heads,
    group,
    q_hbm,
    k_hbm,
    v_hbm,
    stream_hbm,
    seg_hbm,
    arrived_ref,
    inverse_ref,
    q_ref,
    k_ref,
    v_ref,
    stream_ref,
    seg_ref,
    advanced,
    square_out,
    square_in,
    qa,
    own,
    passing,
    buf,
    m_ref,
    acc,
    recv_sem,
    sendz_sem,
    sendx_sem,
    pass_recv_sem,
    pass_send_sem,
    load_sem,
    pipe_send_sem,
    pipe_recv_sem,
    square_send_sem,
    square_recv_sem,
):
    rows = q_ref.shape[0]
    pipe = lax.axis_index("pipe")
    n_pipe = lax.axis_size("pipe")
    tp = lax.axis_index("tp")
    n_tp = lax.axis_size("tp")
    following = (pipe + 1) % n_pipe
    preceding = (pipe + n_pipe - 1) % n_pipe
    ctx = lax.axis_index("ctx")
    n_ctx = lax.axis_size("ctx")
    x = ctx // NZ
    z = ctx % NZ
    right = (ctx + NZ) % n_ctx
    left = (ctx + n_ctx - NZ) % n_ctx

    loads = [
        pltpu.make_async_copy(src, dst, load_sem.at[i])
        for i, (src, dst) in enumerate(
            (
                (seg_hbm, seg_ref),
                (k_hbm, k_ref),
                (v_hbm, v_ref),
                (q_hbm, q_ref),
                (stream_hbm, stream_ref),
            )
        )
    ]
    for load in loads:
        load.start()

    barrier = pltpu.get_barrier_semaphore()
    for peer in (right, left):
        pl.semaphore_signal(barrier, inc=1, device_id={"ctx": peer}, device_id_type=MESH)

    @pl.when(z < NZ - 1)
    def _():
        pl.semaphore_signal(barrier, inc=1, device_id={"ctx": ctx + 1}, device_id_type=MESH)

    @pl.when(z > 0)
    def _():
        pl.semaphore_signal(barrier, inc=1, device_id={"ctx": ctx - 1}, device_id_type=MESH)

    for peer in (following, preceding):
        for half in range(n_tp):
            pl.semaphore_signal(
                barrier, inc=1, device_id={"pipe": peer, "tp": half}, device_id_type=MESH
            )

    def part(h):
        if h == 0:
            return pl.ds(0, OH_ROWS + 2 * HEAD)
        return pl.ds(OH_ROWS + 2 * HEAD * h, 2 * HEAD)

    def send(src, dst, h, send_sem, arrive_sem, peer):
        return pltpu.make_async_remote_copy(
            src_ref=src.at[part(h), :],
            dst_ref=dst.at[part(h), :],
            send_sem=send_sem,
            recv_sem=arrive_sem,
            device_id={"ctx": peer},
            device_id_type=MESH,
        )

    def copy_of(src, slot, which, h, send_sem, peer):
        return send(src, buf.at[slot, which], h, send_sem, recv_sem.at[slot, which, h], peer)

    def up(h):
        return copy_of(own, z, 0, h, sendz_sem.at[NZ, h], ctx + 1)

    def across(h):
        return copy_of(own, z, 0, h, sendx_sem.at[NZ, h], right)

    def pass_first(h):
        return send(own, passing, h, pass_send_sem.at[0, h], pass_recv_sem.at[h], left)

    def pass_second(h):
        return copy_of(passing, z, 1, h, pass_send_sem.at[1, h], left)

    for load in loads[:3]:
        load.wait()
    seg_f = seg_ref[...].astype(jnp.float32)
    doc_rows = lax.broadcasted_iota(jnp.int32, (OH_ROWS, rows), 0).astype(jnp.float32)
    own[0:OH_ROWS, :] = jnp.where(
        doc_rows == jnp.broadcast_to(seg_f, (OH_ROWS, rows)), 1.0, 0.0
    ).astype(jnp.bfloat16)
    for h in range(kv_heads):
        base = OH_ROWS + 2 * HEAD * h
        key_block = k_ref[:, h * HEAD : (h + 1) * HEAD].astype(jnp.float32)
        own[base : base + HEAD, :] = key_block.T.astype(jnp.bfloat16)
        own[base + HEAD : base + 2 * HEAD, :] = v_ref[:, h * HEAD : (h + 1) * HEAD]
        if h == 0:
            pl.semaphore_wait(
                barrier,
                2 + 2 * n_tp + jnp.where(z < NZ - 1, 1, 0) + jnp.where(z > 0, 1, 0),
            )
        across(h).start()

        @pl.when(z < NZ - 1)
        def _():
            up(h).start()

        pass_first(h).start()

    scale = LOG2E * HEAD ** (-0.5)
    height = group * rows
    ones = jnp.ones((2 * rows, HEAD), jnp.bfloat16)
    pad = jnp.zeros((HEAD - OH_ROWS, 2 * rows), jnp.bfloat16)

    causal = lax.broadcasted_iota(jnp.int32, (height, rows), 0) % rows >= lax.broadcasted_iota(
        jnp.int32, (height, rows), 1
    )

    def attend_own(h):
        base = OH_ROWS + 2 * HEAD * h
        rhs = jnp.concatenate(
            [own[base : base + HEAD, :], own[0:OH_ROWS, :], pad[:, 0:rows]], axis=0
        )
        s = jnp.dot(qa[h], rhs, preferred_element_type=jnp.float32)
        s = jnp.where(causal, s, -FAR)
        top = jnp.broadcast_to(jnp.max(s, axis=1, keepdims=True), (height, HEAD))
        p = jnp.exp2((s - top) * scale).astype(jnp.bfloat16)
        va = jnp.concatenate([own[base + HEAD : base + 2 * HEAD, :], ones[0:rows]], axis=1)
        m_ref[h] = top
        acc[h] = jnp.dot(p, va, preferred_element_type=jnp.float32)

    nowhere = jnp.where(
        lax.broadcasted_iota(jnp.int32, (OH_ROWS, rows), 0) == OH_ROWS - 1, 1.0, 0.0
    ).astype(jnp.bfloat16)

    both = jnp.minimum(z, NZ - z)

    def place(t):
        paired = jnp.where(t <= 2 * both, 1, 0)
        r = paired * ((t + 1) // 2) + (1 - paired) * (t - both)
        tall = jnp.where(z > NZ - z, 0, 1)
        k = paired * (t % 2) + (1 - paired) * tall
        slot = (1 - k) * (z - r) + k * (z + r - 1)
        onward = (1 - k) * (NZ - 1 - z) + k * z > 0
        first_of_beyond = r + NZ * (1 - k) == 1
        return slot, k, onward, first_of_beyond

    def forward_z(slot, k, h):
        return copy_of(buf.at[slot, 0], slot, 0, h, sendz_sem.at[slot, h], ctx + 1 - 2 * k)

    def forward_x(slot, h):
        return copy_of(buf.at[slot, 0], slot, 1, h, sendx_sem.at[slot, h], right)

    def relay(at, h):
        slot, k, onward, first_of_beyond = at
        across_wait = copy_of(buf.at[slot, 0], slot, 0, h, sendz_sem.at[slot, h], right)
        across_wait.wait_recv()

        @pl.when(onward)
        def _():
            forward_z(slot, k, h).start()

        @pl.when(jnp.logical_not(first_of_beyond))
        def _():
            forward_x(slot, h).start()

    def attend(at, h):
        slot, k, _, _ = at
        forward_x(slot, h).wait_recv()
        oh0 = jnp.where(x >= k, buf[slot, 0, 0:OH_ROWS, :], nowhere)
        oh1 = jnp.where(x >= k + 1, buf[slot, 1, 0:OH_ROWS, :], nowhere)
        oh = jnp.concatenate([oh0, oh1], axis=1)
        base = OH_ROWS + 2 * HEAD * h
        kt = jnp.concatenate(
            [buf[slot, 0, base : base + HEAD, :], buf[slot, 1, base : base + HEAD, :]],
            axis=1,
        )
        rhs = jnp.concatenate([kt, oh, pad], axis=0)
        s = jnp.dot(qa[h], rhs, preferred_element_type=jnp.float32)
        old = m_ref[h]
        top = jnp.maximum(old, jnp.max(s, axis=1, keepdims=True))
        p = jnp.exp2((s - jnp.concatenate([top, top], axis=1)) * scale)
        fade = jnp.exp2((old - top) * scale)
        vals = jnp.concatenate(
            [
                buf[slot, 0, base + HEAD : base + 2 * HEAD, :],
                buf[slot, 1, base + HEAD : base + 2 * HEAD, :],
            ],
            axis=0,
        )
        va = jnp.concatenate([vals, ones], axis=1)
        m_ref[h] = top
        acc[h] = acc[h] * jnp.concatenate([fade, fade], axis=1) + jnp.dot(
            p.astype(jnp.bfloat16), va, preferred_element_type=jnp.float32
        )

    first = place(1)
    for h in range(kv_heads):
        pass_first(h).wait_recv()
        pass_second(h).start()
        relay(first, h)

    loads[3].wait()
    seg_col = jnp.broadcast_to(seg_f, (rows, rows)).T
    lane = lax.broadcasted_iota(jnp.int32, (rows, HEAD), 1)
    penalty = jnp.where(
        (lane < OH_ROWS) & (lane.astype(jnp.float32) != seg_col), -FAR, 0.0
    ).astype(jnp.bfloat16)
    for h in range(kv_heads):
        for g in range(group):
            c = (h * group + g) * HEAD
            qa[h, g * rows : (g + 1) * rows, 0:HEAD] = q_ref[:, c : c + HEAD]
            qa[h, g * rows : (g + 1) * rows, HEAD : 2 * HEAD] = penalty

    def step(t, carry):
        now, before = place(t), place(t - LAG)
        for h in range(kv_heads):
            relay(now, h)
            attend(before, h)
        return carry

    def step_without(t, carry):
        now = place(t)
        for h in range(kv_heads):
            relay(now, h)
        return carry

    def step_own(t, carry):
        now = place(t)
        for h in range(kv_heads):
            relay(now, h)
            attend_own(h)
        return carry

    lax.fori_loop(2, LAG, step_without, 0)
    lax.fori_loop(LAG, LAG + 1, step_own, 0)
    lax.fori_loop(LAG + 1, NZ + 1, step, 0)

    loads[4].wait()
    width = group * HEAD

    def relay_out(h):
        columns = pl.ds(h * width, width)
        return pltpu.make_async_remote_copy(
            src_ref=advanced.at[:, columns],
            dst_ref=arrived_ref.at[:, columns],
            send_sem=pipe_send_sem.at[h],
            recv_sem=pipe_recv_sem.at[h],
            device_id={"pipe": following},
            device_id_type=MESH,
        )

    squares = jnp.zeros((rows, HEAD), jnp.float32)
    for h in range(kv_heads):

        def rest(t, carry):
            attend(place(t), h)
            return carry

        lax.fori_loop(NZ - LAG + 1, NZ + 1, rest, 0)
        for g in range(group):
            c = (h * group + g) * HEAD
            top_rows = slice(g * rows, (g + 1) * rows)
            mixed = acc[h, top_rows, 0:HEAD] / acc[h, top_rows, HEAD : 2 * HEAD]
            mixed = mixed.astype(jnp.bfloat16).astype(jnp.float32)
            total = (stream_ref[:, c : c + HEAD].astype(jnp.float32) + mixed).astype(jnp.bfloat16)
            advanced[:, c : c + HEAD] = total
            wide = total.astype(jnp.float32)
            squares = squares + wide * wide
        relay_out(h).start()
    row_sums = jnp.broadcast_to(jnp.sum(squares, axis=1, keepdims=True), (rows, HEAD))
    square_out[...] = row_sums.T[0:8, :]

    def sums_out(t):
        return pltpu.make_async_remote_copy(
            src_ref=square_out,
            dst_ref=square_in.at[t],
            send_sem=square_send_sem.at[t],
            recv_sem=square_recv_sem.at[t],
            device_id={"pipe": following, "tp": (tp + t) % n_tp},
            device_id_type=MESH,
        )

    for t in range(n_tp):
        sums_out(n_tp - 1 - t).start()

    for h in range(kv_heads):
        across(h).wait_send()
        pass_first(h).wait_send()
        pass_second(h).wait_send()

        @pl.when(z < NZ - 1)
        def _():
            up(h).wait_send()

    def drain(t, carry):
        slot, k, onward, first_of_beyond = place(t)
        for h in range(kv_heads):

            @pl.when(onward)
            def _():
                forward_z(slot, k, h).wait_send()

            @pl.when(jnp.logical_not(first_of_beyond))
            def _():
                forward_x(slot, h).wait_send()

        return carry

    lax.fori_loop(1, NZ + 1, drain, 0)

    for t in range(n_tp):
        sums_out(t).wait_recv()
    total = square_in[0, 0:1, :]
    for t in range(1, n_tp):
        total = total + square_in[t, 0:1, :]
    inverse = lax.rsqrt(total / (QUERY_HEADS * HEAD) + 1e-05)
    inverse_ref[...] = jnp.broadcast_to(inverse, (rows, rows)).T
    for h in range(kv_heads):
        relay_out(h).wait_recv()
    for h in range(kv_heads):
        relay_out(h).wait_send()
    for t in range(n_tp):
        sums_out(t).wait_send()


def norm_kernel(in_ref, inverse_ref, gain_ref, arrived_ref, normed_ref):
    inverse = inverse_ref[...]
    for c in range(0, in_ref.shape[1], HEAD):
        block = in_ref[:, c : c + HEAD]
        arrived_ref[:, c : c + HEAD] = block
        gain = gain_ref[c : c + HEAD].astype(jnp.float32)[None, :]
        normed_ref[:, c : c + HEAD] = (block.astype(jnp.float32) * inverse * gain).astype(
            jnp.bfloat16
        )


def per_device(stream, queries, keys, values, segments, norm_gain):
    stream, queries, keys, values = stream[0], queries[0], keys[0], values[0]
    rows = queries.shape[0]
    kv_heads = keys.shape[1] // HEAD
    group = queries.shape[1] // keys.shape[1]
    block_rows = OH_ROWS + 2 * HEAD * kv_heads
    n_tp = lax.axis_size("tp")
    vmem = pl.BlockSpec(memory_space=pltpu.VMEM)
    anywhere = pl.BlockSpec(memory_space=pltpu.HBM)
    like_stream = jax.ShapeDtypeStruct(stream.shape, jnp.bfloat16)
    arrived, inverse = pl.pallas_call(
        functools.partial(attention_kernel, kv_heads, group),
        out_shape=(like_stream, jax.ShapeDtypeStruct((rows, HEAD), jnp.float32)),
        in_specs=[anywhere] * 5,
        out_specs=(vmem, vmem),
        scratch_shapes=[
            pltpu.VMEM(queries.shape, jnp.bfloat16),
            pltpu.VMEM(keys.shape, jnp.bfloat16),
            pltpu.VMEM(values.shape, jnp.bfloat16),
            pltpu.VMEM(stream.shape, jnp.bfloat16),
            pltpu.VMEM(segments.shape, segments.dtype),
            pltpu.VMEM(stream.shape, jnp.bfloat16),
            pltpu.VMEM((8, rows), jnp.float32),
            pltpu.VMEM((n_tp, 8, rows), jnp.float32),
            pltpu.VMEM((kv_heads, group * rows, 2 * HEAD), jnp.bfloat16),
            pltpu.VMEM((block_rows, rows), jnp.bfloat16),
            pltpu.VMEM((block_rows, rows), jnp.bfloat16),
            pltpu.VMEM((NZ, 2, block_rows, rows), jnp.bfloat16),
            pltpu.VMEM((kv_heads, group * rows, HEAD), jnp.float32),
            pltpu.VMEM((kv_heads, group * rows, 2 * HEAD), jnp.float32),
            pltpu.SemaphoreType.DMA((NZ, 2, kv_heads)),
            pltpu.SemaphoreType.DMA((NZ + 1, kv_heads)),
            pltpu.SemaphoreType.DMA((NZ + 1, kv_heads)),
            pltpu.SemaphoreType.DMA((kv_heads,)),
            pltpu.SemaphoreType.DMA((2, kv_heads)),
            pltpu.SemaphoreType.DMA((5,)),
            pltpu.SemaphoreType.DMA((kv_heads,)),
            pltpu.SemaphoreType.DMA((kv_heads,)),
            pltpu.SemaphoreType.DMA((n_tp,)),
            pltpu.SemaphoreType.DMA((n_tp,)),
        ],
        compiler_params=pltpu.CompilerParams(
            collective_id=0, has_side_effects=True, vmem_limit_bytes=63 * 1024 * 1024
        ),
    )(queries, keys, values, stream, segments)
    columns = NORM_COLUMNS
    tile = pl.BlockSpec((rows, columns), lambda i: (0, i))
    arrived, normed = pl.pallas_call(
        norm_kernel,
        grid=(stream.shape[1] // columns,),
        out_shape=(like_stream, like_stream),
        in_specs=[
            tile,
            pl.BlockSpec((rows, HEAD), lambda i: (0, 0)),
            pl.BlockSpec((columns,), lambda i: (i,)),
        ],
        out_specs=(tile, tile),
    )(arrived, inverse, norm_gain)
    return (arrived[None], normed[None])


def solution(mesh):
    in_specs = (
        P("pipe", "ctx", "tp"),
        P("pipe", "ctx", "tp"),
        P("pipe", "ctx", "tp"),
        P("pipe", "ctx", "tp"),
        P("pipe", "ctx"),
        P("tp"),
    )
    out_specs = (P("pipe", "ctx", "tp"), P("pipe", "ctx", "tp"))
    return jax.shard_map(
        per_device, mesh=mesh, in_specs=in_specs, out_specs=out_specs, check_vma=False
    )
```

```python
import functools

import jax
import jax.numpy as jnp
from jax import lax
from jax.experimental import pallas as pl
from jax.experimental.pallas import tpu as pltpu
from jax.sharding import PartitionSpec as P

QUERY_HEADS = 32
HEAD = 128
MESH = pl.DeviceIdType.MESH
NZ = 8
OH_ROWS = 16
NORM_COLUMNS = 1024
LAG = 3
FAR = float(2**20)
LOG2E = 1.4426950408889634


def attention_kernel(
    kv_heads,
    group,
    q_hbm,
    k_hbm,
    v_hbm,
    stream_hbm,
    seg_hbm,
    arrived_ref,
    inverse_ref,
    q_ref,
    k_ref,
    v_ref,
    stream_ref,
    seg_ref,
    advanced,
    square_out,
    square_in,
    qa,
    own,
    passing,
    buf,
    m_ref,
    acc,
    recv_sem,
    sendz_sem,
    sendx_sem,
    pass_recv_sem,
    pass_send_sem,
    load_sem,
    pipe_send_sem,
    pipe_recv_sem,
    square_send_sem,
    square_recv_sem,
):
    rows = q_ref.shape[0]
    pipe = lax.axis_index("pipe")
    n_pipe = lax.axis_size("pipe")
    tp = lax.axis_index("tp")
    n_tp = lax.axis_size("tp")
    following = (pipe + 1) % n_pipe
    preceding = (pipe + n_pipe - 1) % n_pipe
    ctx = lax.axis_index("ctx")
    n_ctx = lax.axis_size("ctx")
    x = ctx // NZ
    z = ctx % NZ
    right = (ctx + NZ) % n_ctx
    left = (ctx + n_ctx - NZ) % n_ctx

    loads = [
        pltpu.make_async_copy(src, dst, load_sem.at[i])
        for i, (src, dst) in enumerate(
            (
                (seg_hbm, seg_ref),
                (k_hbm, k_ref),
                (v_hbm, v_ref),
                (q_hbm, q_ref),
                (stream_hbm, stream_ref),
            )
        )
    ]
    for load in loads:
        load.start()

    barrier = pltpu.get_barrier_semaphore()
    for peer in (right, left):
        pl.semaphore_signal(barrier, inc=1, device_id={"ctx": peer}, device_id_type=MESH)

    @pl.when(z < NZ - 1)
    def _():
        pl.semaphore_signal(barrier, inc=1, device_id={"ctx": ctx + 1}, device_id_type=MESH)

    @pl.when(z > 0)
    def _():
        pl.semaphore_signal(barrier, inc=1, device_id={"ctx": ctx - 1}, device_id_type=MESH)

    for peer in (following, preceding):
        for half in range(n_tp):
            pl.semaphore_signal(
                barrier, inc=1, device_id={"pipe": peer, "tp": half}, device_id_type=MESH
            )

    def part(h):
        if h == 0:
            return pl.ds(0, OH_ROWS + 2 * HEAD)
        return pl.ds(OH_ROWS + 2 * HEAD * h, 2 * HEAD)

    def send(src, dst, h, send_sem, arrive_sem, peer):
        return pltpu.make_async_remote_copy(
            src_ref=src.at[part(h), :],
            dst_ref=dst.at[part(h), :],
            send_sem=send_sem,
            recv_sem=arrive_sem,
            device_id={"ctx": peer},
            device_id_type=MESH,
        )

    def copy_of(src, slot, which, h, send_sem, peer):
        return send(src, buf.at[slot, which], h, send_sem, recv_sem.at[slot, which, h], peer)

    def up(h):
        return copy_of(own, z, 0, h, sendz_sem.at[NZ, h], ctx + 1)

    def across(h):
        return copy_of(own, z, 0, h, sendx_sem.at[NZ, h], right)

    def pass_first(h):
        return send(own, passing, h, pass_send_sem.at[0, h], pass_recv_sem.at[h], left)

    def pass_second(h):
        return copy_of(passing, z, 1, h, pass_send_sem.at[1, h], left)

    for load in loads[:3]:
        load.wait()
    seg_f = seg_ref[...].astype(jnp.float32)
    doc_rows = lax.broadcasted_iota(jnp.int32, (OH_ROWS, rows), 0).astype(jnp.float32)
    own[0:OH_ROWS, :] = jnp.where(
        doc_rows == jnp.broadcast_to(seg_f, (OH_ROWS, rows)), 1.0, 0.0
    ).astype(jnp.bfloat16)
    for h in range(kv_heads):
        base = OH_ROWS + 2 * HEAD * h
        key_block = k_ref[:, h * HEAD : (h + 1) * HEAD].astype(jnp.float32)
        own[base : base + HEAD, :] = key_block.T.astype(jnp.bfloat16)
        own[base + HEAD : base + 2 * HEAD, :] = v_ref[:, h * HEAD : (h + 1) * HEAD]
        if h == 0:
            pl.semaphore_wait(
                barrier,
                2 + 2 * n_tp + jnp.where(z < NZ - 1, 1, 0) + jnp.where(z > 0, 1, 0),
            )
        across(h).start()

        @pl.when(z < NZ - 1)
        def _():
            up(h).start()

        pass_first(h).start()

    scale = LOG2E * HEAD ** (-0.5)
    height = group * rows
    ones = jnp.ones((2 * rows, HEAD), jnp.bfloat16)
    pad = jnp.zeros((HEAD - OH_ROWS, 2 * rows), jnp.bfloat16)

    causal = lax.broadcasted_iota(jnp.int32, (height, rows), 0) % rows >= lax.broadcasted_iota(
        jnp.int32, (height, rows), 1
    )

    def attend_own(h):
        base = OH_ROWS + 2 * HEAD * h
        rhs = jnp.concatenate(
            [own[base : base + HEAD, :], own[0:OH_ROWS, :], pad[:, 0:rows]], axis=0
        )
        s = jnp.dot(qa[h], rhs, preferred_element_type=jnp.float32)
        s = jnp.where(causal, s, -FAR)
        top = jnp.broadcast_to(jnp.max(s, axis=1, keepdims=True), (height, HEAD))
        p = jnp.exp2((s - top) * scale).astype(jnp.bfloat16)
        va = jnp.concatenate([own[base + HEAD : base + 2 * HEAD, :], ones[0:rows]], axis=1)
        m_ref[h] = top
        acc[h] = jnp.dot(p, va, preferred_element_type=jnp.float32)

    nowhere = jnp.where(
        lax.broadcasted_iota(jnp.int32, (OH_ROWS, rows), 0) == OH_ROWS - 1, 1.0, 0.0
    ).astype(jnp.bfloat16)

    both = jnp.minimum(z, NZ - z)

    def place(t):
        paired = jnp.where(t <= 2 * both, 1, 0)
        r = paired * ((t + 1) // 2) + (1 - paired) * (t - both)
        tall = jnp.where(z > NZ - z, 0, 1)
        k = paired * (t % 2) + (1 - paired) * tall
        slot = (1 - k) * (z - r) + k * (z + r - 1)
        onward = (1 - k) * (NZ - 1 - z) + k * z > 0
        first_of_beyond = r + NZ * (1 - k) == 1
        return slot, k, onward, first_of_beyond

    def forward_z(slot, k, h):
        return copy_of(buf.at[slot, 0], slot, 0, h, sendz_sem.at[slot, h], ctx + 1 - 2 * k)

    def forward_x(slot, h):
        return copy_of(buf.at[slot, 0], slot, 1, h, sendx_sem.at[slot, h], right)

    def relay(at, h):
        slot, k, onward, first_of_beyond = at
        across_wait = copy_of(buf.at[slot, 0], slot, 0, h, sendz_sem.at[slot, h], right)
        across_wait.wait_recv()

        @pl.when(onward)
        def _():
            forward_z(slot, k, h).start()

        @pl.when(jnp.logical_not(first_of_beyond))
        def _():
            forward_x(slot, h).start()

    def attend(at, h):
        slot, k, _, _ = at
        forward_x(slot, h).wait_recv()
        oh0 = jnp.where(x >= k, buf[slot, 0, 0:OH_ROWS, :], nowhere)
        oh1 = jnp.where(x >= k + 1, buf[slot, 1, 0:OH_ROWS, :], nowhere)
        oh = jnp.concatenate([oh0, oh1], axis=1)
        base = OH_ROWS + 2 * HEAD * h
        kt = jnp.concatenate(
            [buf[slot, 0, base : base + HEAD, :], buf[slot, 1, base : base + HEAD, :]],
            axis=1,
        )
        rhs = jnp.concatenate([kt, oh, pad], axis=0)
        s = jnp.dot(qa[h], rhs, preferred_element_type=jnp.float32)
        old = m_ref[h]
        top = jnp.maximum(old, jnp.max(s, axis=1, keepdims=True))
        p = jnp.exp2((s - jnp.concatenate([top, top], axis=1)) * scale)
        fade = jnp.exp2((old - top) * scale)
        vals = jnp.concatenate(
            [
                buf[slot, 0, base + HEAD : base + 2 * HEAD, :],
                buf[slot, 1, base + HEAD : base + 2 * HEAD, :],
            ],
            axis=0,
        )
        va = jnp.concatenate([vals, ones], axis=1)
        m_ref[h] = top
        acc[h] = acc[h] * jnp.concatenate([fade, fade], axis=1) + jnp.dot(
            p.astype(jnp.bfloat16), va, preferred_element_type=jnp.float32
        )

    first = place(1)
    for h in range(kv_heads):
        pass_first(h).wait_recv()
        pass_second(h).start()
        relay(first, h)

    loads[3].wait()
    seg_col = jnp.broadcast_to(seg_f, (rows, rows)).T
    lane = lax.broadcasted_iota(jnp.int32, (rows, HEAD), 1)
    penalty = jnp.where(
        (lane < OH_ROWS) & (lane.astype(jnp.float32) != seg_col), -FAR, 0.0
    ).astype(jnp.bfloat16)
    for h in range(kv_heads):
        for g in range(group):
            c = (h * group + g) * HEAD
            qa[h, g * rows : (g + 1) * rows, 0:HEAD] = q_ref[:, c : c + HEAD]
            qa[h, g * rows : (g + 1) * rows, HEAD : 2 * HEAD] = penalty

    def step(t, carry):
        now, before = place(t), place(t - LAG)
        for h in range(kv_heads):
            relay(now, h)
            attend(before, h)
        return carry

    def step_without(t, carry):
        now = place(t)
        for h in range(kv_heads):
            relay(now, h)
        return carry

    def step_own(t, carry):
        now = place(t)
        for h in range(kv_heads):
            relay(now, h)
            attend_own(h)
        return carry

    lax.fori_loop(2, LAG, step_without, 0)
    lax.fori_loop(LAG, LAG + 1, step_own, 0)
    lax.fori_loop(LAG + 1, NZ + 1, step, 0)

    loads[4].wait()
    width = group * HEAD

    def relay_out(h):
        columns = pl.ds(h * width, width)
        return pltpu.make_async_remote_copy(
            src_ref=advanced.at[:, columns],
            dst_ref=arrived_ref.at[:, columns],
            send_sem=pipe_send_sem.at[h],
            recv_sem=pipe_recv_sem.at[h],
            device_id={"pipe": following},
            device_id_type=MESH,
        )

    squares = jnp.zeros((rows, HEAD), jnp.float32)
    for h in range(kv_heads):

        def rest(t, carry):
            attend(place(t), h)
            return carry

        lax.fori_loop(NZ - LAG + 1, NZ + 1, rest, 0)
        for g in range(group):
            c = (h * group + g) * HEAD
            top_rows = slice(g * rows, (g + 1) * rows)
            mixed = acc[h, top_rows, 0:HEAD] / acc[h, top_rows, HEAD : 2 * HEAD]
            mixed = mixed.astype(jnp.bfloat16).astype(jnp.float32)
            total = (stream_ref[:, c : c + HEAD].astype(jnp.float32) + mixed).astype(jnp.bfloat16)
            advanced[:, c : c + HEAD] = total
            wide = total.astype(jnp.float32)
            squares = squares + wide * wide
        if h < kv_heads - 1:
            relay_out(h).start()
    row_sums = jnp.broadcast_to(jnp.sum(squares, axis=1, keepdims=True), (rows, HEAD))
    square_out[...] = row_sums.T[0:8, :]

    def sums_out(t):
        return pltpu.make_async_remote_copy(
            src_ref=square_out,
            dst_ref=square_in.at[t],
            send_sem=square_send_sem.at[t],
            recv_sem=square_recv_sem.at[t],
            device_id={"pipe": following, "tp": (tp + t) % n_tp},
            device_id_type=MESH,
        )

    for t in range(n_tp):
        sums_out(n_tp - 1 - t).start()
    relay_out(kv_heads - 1).start()

    for h in range(kv_heads):
        across(h).wait_send()
        pass_first(h).wait_send()
        pass_second(h).wait_send()

        @pl.when(z < NZ - 1)
        def _():
            up(h).wait_send()

    def drain(t, carry):
        slot, k, onward, first_of_beyond = place(t)
        for h in range(kv_heads):

            @pl.when(onward)
            def _():
                forward_z(slot, k, h).wait_send()

            @pl.when(jnp.logical_not(first_of_beyond))
            def _():
                forward_x(slot, h).wait_send()

        return carry

    lax.fori_loop(1, NZ + 1, drain, 0)

    for t in range(n_tp):
        sums_out(t).wait_recv()
    total = square_in[0, 0:1, :]
    for t in range(1, n_tp):
        total = total + square_in[t, 0:1, :]
    inverse = lax.rsqrt(total / (QUERY_HEADS * HEAD) + 1e-05)
    inverse_ref[...] = jnp.broadcast_to(inverse, (rows, rows)).T
    for h in range(kv_heads):
        relay_out(h).wait_recv()
    for h in range(kv_heads):
        relay_out(h).wait_send()
    for t in range(n_tp):
        sums_out(t).wait_send()


def norm_kernel(in_ref, inverse_ref, gain_ref, arrived_ref, normed_ref):
    inverse = inverse_ref[...]
    for c in range(0, in_ref.shape[1], HEAD):
        block = in_ref[:, c : c + HEAD]
        arrived_ref[:, c : c + HEAD] = block
        gain = gain_ref[c : c + HEAD].astype(jnp.float32)[None, :]
        normed_ref[:, c : c + HEAD] = (block.astype(jnp.float32) * inverse * gain).astype(
            jnp.bfloat16
        )


def per_device(stream, queries, keys, values, segments, norm_gain):
    stream, queries, keys, values = stream[0], queries[0], keys[0], values[0]
    rows = queries.shape[0]
    kv_heads = keys.shape[1] // HEAD
    group = queries.shape[1] // keys.shape[1]
    block_rows = OH_ROWS + 2 * HEAD * kv_heads
    n_tp = lax.axis_size("tp")
    vmem = pl.BlockSpec(memory_space=pltpu.VMEM)
    anywhere = pl.BlockSpec(memory_space=pltpu.HBM)
    like_stream = jax.ShapeDtypeStruct(stream.shape, jnp.bfloat16)
    arrived, inverse = pl.pallas_call(
        functools.partial(attention_kernel, kv_heads, group),
        out_shape=(like_stream, jax.ShapeDtypeStruct((rows, HEAD), jnp.float32)),
        in_specs=[anywhere] * 5,
        out_specs=(vmem, vmem),
        scratch_shapes=[
            pltpu.VMEM(queries.shape, jnp.bfloat16),
            pltpu.VMEM(keys.shape, jnp.bfloat16),
            pltpu.VMEM(values.shape, jnp.bfloat16),
            pltpu.VMEM(stream.shape, jnp.bfloat16),
            pltpu.VMEM(segments.shape, segments.dtype),
            pltpu.VMEM(stream.shape, jnp.bfloat16),
            pltpu.VMEM((8, rows), jnp.float32),
            pltpu.VMEM((n_tp, 8, rows), jnp.float32),
            pltpu.VMEM((kv_heads, group * rows, 2 * HEAD), jnp.bfloat16),
            pltpu.VMEM((block_rows, rows), jnp.bfloat16),
            pltpu.VMEM((block_rows, rows), jnp.bfloat16),
            pltpu.VMEM((NZ, 2, block_rows, rows), jnp.bfloat16),
            pltpu.VMEM((kv_heads, group * rows, HEAD), jnp.float32),
            pltpu.VMEM((kv_heads, group * rows, 2 * HEAD), jnp.float32),
            pltpu.SemaphoreType.DMA((NZ, 2, kv_heads)),
            pltpu.SemaphoreType.DMA((NZ + 1, kv_heads)),
            pltpu.SemaphoreType.DMA((NZ + 1, kv_heads)),
            pltpu.SemaphoreType.DMA((kv_heads,)),
            pltpu.SemaphoreType.DMA((2, kv_heads)),
            pltpu.SemaphoreType.DMA((5,)),
            pltpu.SemaphoreType.DMA((kv_heads,)),
            pltpu.SemaphoreType.DMA((kv_heads,)),
            pltpu.SemaphoreType.DMA((n_tp,)),
            pltpu.SemaphoreType.DMA((n_tp,)),
        ],
        compiler_params=pltpu.CompilerParams(
            collective_id=0, has_side_effects=True, vmem_limit_bytes=63 * 1024 * 1024
        ),
    )(queries, keys, values, stream, segments)
    columns = NORM_COLUMNS
    tile = pl.BlockSpec((rows, columns), lambda i: (0, i))
    arrived, normed = pl.pallas_call(
        norm_kernel,
        grid=(stream.shape[1] // columns,),
        out_shape=(like_stream, like_stream),
        in_specs=[
            tile,
            pl.BlockSpec((rows, HEAD), lambda i: (0, 0)),
            pl.BlockSpec((columns,), lambda i: (i,)),
        ],
        out_specs=(tile, tile),
    )(arrived, inverse, norm_gain)
    return (arrived[None], normed[None])


def solution(mesh):
    in_specs = (
        P("pipe", "ctx", "tp"),
        P("pipe", "ctx", "tp"),
        P("pipe", "ctx", "tp"),
        P("pipe", "ctx", "tp"),
        P("pipe", "ctx"),
        P("tp"),
    )
    out_specs = (P("pipe", "ctx", "tp"), P("pipe", "ctx", "tp"))
    return jax.shard_map(
        per_device, mesh=mesh, in_specs=in_specs, out_specs=out_specs, check_vma=False
    )
```

```python
import functools

import jax
import jax.numpy as jnp
from jax import lax
from jax.experimental import pallas as pl
from jax.experimental.pallas import tpu as pltpu
from jax.sharding import PartitionSpec as P

QUERY_HEADS = 32
HEAD = 128
MESH = pl.DeviceIdType.MESH
NZ = 8
OH_ROWS = 16
NORM_COLUMNS = 1024
LAG = 3
FAR = float(2**20)
LOG2E = 1.4426950408889634


def attention_kernel(
    kv_heads,
    group,
    q_hbm,
    k_hbm,
    v_hbm,
    stream_hbm,
    seg_hbm,
    arrived_ref,
    inverse_ref,
    q_ref,
    k_ref,
    v_ref,
    stream_ref,
    seg_ref,
    advanced,
    square_out,
    square_in,
    qa,
    own,
    passing,
    buf,
    m_ref,
    acc,
    recv_sem,
    sendz_sem,
    sendx_sem,
    pass_recv_sem,
    pass_send_sem,
    load_sem,
    pipe_send_sem,
    pipe_recv_sem,
    square_send_sem,
    square_recv_sem,
):
    rows = q_ref.shape[0]
    pipe = lax.axis_index("pipe")
    n_pipe = lax.axis_size("pipe")
    tp = lax.axis_index("tp")
    n_tp = lax.axis_size("tp")
    following = (pipe + 1) % n_pipe
    preceding = (pipe + n_pipe - 1) % n_pipe
    ctx = lax.axis_index("ctx")
    n_ctx = lax.axis_size("ctx")
    x = ctx // NZ
    z = ctx % NZ
    right = (ctx + NZ) % n_ctx
    left = (ctx + n_ctx - NZ) % n_ctx

    loads = [
        pltpu.make_async_copy(src, dst, load_sem.at[i])
        for i, (src, dst) in enumerate(
            (
                (seg_hbm, seg_ref),
                (k_hbm, k_ref),
                (v_hbm, v_ref),
                (q_hbm, q_ref),
                (stream_hbm, stream_ref),
            )
        )
    ]
    for load in loads:
        load.start()

    barrier = pltpu.get_barrier_semaphore()
    for peer in (right, left):
        pl.semaphore_signal(barrier, inc=1, device_id={"ctx": peer}, device_id_type=MESH)

    @pl.when(z < NZ - 1)
    def _():
        pl.semaphore_signal(barrier, inc=1, device_id={"ctx": ctx + 1}, device_id_type=MESH)

    @pl.when(z > 0)
    def _():
        pl.semaphore_signal(barrier, inc=1, device_id={"ctx": ctx - 1}, device_id_type=MESH)

    for peer in (following, preceding):
        for half in range(n_tp):
            pl.semaphore_signal(
                barrier, inc=1, device_id={"pipe": peer, "tp": half}, device_id_type=MESH
            )

    def part(h):
        if h == 0:
            return pl.ds(0, OH_ROWS + 2 * HEAD)
        return pl.ds(OH_ROWS + 2 * HEAD * h, 2 * HEAD)

    def send(src, dst, h, send_sem, arrive_sem, peer):
        return pltpu.make_async_remote_copy(
            src_ref=src.at[part(h), :],
            dst_ref=dst.at[part(h), :],
            send_sem=send_sem,
            recv_sem=arrive_sem,
            device_id={"ctx": peer},
            device_id_type=MESH,
        )

    def copy_of(src, slot, which, h, send_sem, peer):
        return send(src, buf.at[slot, which], h, send_sem, recv_sem.at[slot, which, h], peer)

    def up(h):
        return copy_of(own, z, 0, h, sendz_sem.at[NZ, h], ctx + 1)

    def across(h):
        return copy_of(own, z, 0, h, sendx_sem.at[NZ, h], right)

    def pass_first(h):
        return send(own, passing, h, pass_send_sem.at[0, h], pass_recv_sem.at[h], left)

    def pass_second(h):
        return copy_of(passing, z, 1, h, pass_send_sem.at[1, h], left)

    for load in loads[:3]:
        load.wait()
    seg_f = seg_ref[...].astype(jnp.float32)
    doc_rows = lax.broadcasted_iota(jnp.int32, (OH_ROWS, rows), 0).astype(jnp.float32)
    own[0:OH_ROWS, :] = jnp.where(
        doc_rows == jnp.broadcast_to(seg_f, (OH_ROWS, rows)), 1.0, 0.0
    ).astype(jnp.bfloat16)
    for h in range(kv_heads):
        base = OH_ROWS + 2 * HEAD * h
        key_block = k_ref[:, h * HEAD : (h + 1) * HEAD].astype(jnp.float32)
        own[base : base + HEAD, :] = key_block.T.astype(jnp.bfloat16)
        own[base + HEAD : base + 2 * HEAD, :] = v_ref[:, h * HEAD : (h + 1) * HEAD]
        if h == 0:
            pl.semaphore_wait(
                barrier,
                2 + 2 * n_tp + jnp.where(z < NZ - 1, 1, 0) + jnp.where(z > 0, 1, 0),
            )
        across(h).start()

        @pl.when(z < NZ - 1)
        def _():
            up(h).start()

        pass_first(h).start()

    scale = LOG2E * HEAD ** (-0.5)
    height = group * rows
    ones = jnp.ones((2 * rows, HEAD), jnp.bfloat16)
    pad = jnp.zeros((HEAD - OH_ROWS, 2 * rows), jnp.bfloat16)

    causal = lax.broadcasted_iota(jnp.int32, (height, rows), 0) % rows >= lax.broadcasted_iota(
        jnp.int32, (height, rows), 1
    )

    def attend_own(h):
        base = OH_ROWS + 2 * HEAD * h
        rhs = jnp.concatenate(
            [own[base : base + HEAD, :], own[0:OH_ROWS, :], pad[:, 0:rows]], axis=0
        )
        s = jnp.dot(qa[h], rhs, preferred_element_type=jnp.float32)
        s = jnp.where(causal, s, -FAR)
        top = jnp.broadcast_to(jnp.max(s, axis=1, keepdims=True), (height, HEAD))
        p = jnp.exp2((s - top) * scale).astype(jnp.bfloat16)
        va = jnp.concatenate([own[base + HEAD : base + 2 * HEAD, :], ones[0:rows]], axis=1)
        m_ref[h] = top
        acc[h] = jnp.dot(p, va, preferred_element_type=jnp.float32)

    nowhere = jnp.where(
        lax.broadcasted_iota(jnp.int32, (OH_ROWS, rows), 0) == OH_ROWS - 1, 1.0, 0.0
    ).astype(jnp.bfloat16)

    both = jnp.minimum(z, NZ - z)

    def place(t):
        paired = jnp.where(t <= 2 * both, 1, 0)
        r = paired * ((t + 1) // 2) + (1 - paired) * (t - both)
        tall = jnp.where(z > NZ - z, 0, 1)
        k = paired * (t % 2) + (1 - paired) * tall
        slot = (1 - k) * (z - r) + k * (z + r - 1)
        onward = (1 - k) * (NZ - 1 - z) + k * z > 0
        first_of_beyond = r + NZ * (1 - k) == 1
        return slot, k, onward, first_of_beyond

    def forward_z(slot, k, h):
        return copy_of(buf.at[slot, 0], slot, 0, h, sendz_sem.at[slot, h], ctx + 1 - 2 * k)

    def forward_x(slot, h):
        return copy_of(buf.at[slot, 0], slot, 1, h, sendx_sem.at[slot, h], right)

    def relay(at, h):
        slot, k, onward, first_of_beyond = at
        across_wait = copy_of(buf.at[slot, 0], slot, 0, h, sendz_sem.at[slot, h], right)
        across_wait.wait_recv()

        @pl.when(onward)
        def _():
            forward_z(slot, k, h).start()

        @pl.when(jnp.logical_not(first_of_beyond))
        def _():
            forward_x(slot, h).start()

    def attend(at, h):
        slot, k, _, _ = at
        forward_x(slot, h).wait_recv()
        oh0 = jnp.where(x >= k, buf[slot, 0, 0:OH_ROWS, :], nowhere)
        oh1 = jnp.where(x >= k + 1, buf[slot, 1, 0:OH_ROWS, :], nowhere)
        oh = jnp.concatenate([oh0, oh1], axis=1)
        base = OH_ROWS + 2 * HEAD * h
        kt = jnp.concatenate(
            [buf[slot, 0, base : base + HEAD, :], buf[slot, 1, base : base + HEAD, :]],
            axis=1,
        )
        rhs = jnp.concatenate([kt, oh, pad], axis=0)
        s = jnp.dot(qa[h], rhs, preferred_element_type=jnp.float32)
        old = m_ref[h]
        top = jnp.maximum(old, jnp.max(s, axis=1, keepdims=True))
        p = jnp.exp2((s - jnp.concatenate([top, top], axis=1)) * scale)
        fade = jnp.exp2((old - top) * scale)
        vals = jnp.concatenate(
            [
                buf[slot, 0, base + HEAD : base + 2 * HEAD, :],
                buf[slot, 1, base + HEAD : base + 2 * HEAD, :],
            ],
            axis=0,
        )
        va = jnp.concatenate([vals, ones], axis=1)
        m_ref[h] = top
        acc[h] = acc[h] * jnp.concatenate([fade, fade], axis=1) + jnp.dot(
            p.astype(jnp.bfloat16), va, preferred_element_type=jnp.float32
        )

    first = place(1)
    for h in range(kv_heads):
        pass_first(h).wait_recv()
        pass_second(h).start()
        relay(first, h)

    loads[3].wait()
    seg_col = jnp.broadcast_to(seg_f, (rows, rows)).T
    lane = lax.broadcasted_iota(jnp.int32, (rows, HEAD), 1)
    penalty = jnp.where(
        (lane < OH_ROWS) & (lane.astype(jnp.float32) != seg_col), -FAR, 0.0
    ).astype(jnp.bfloat16)
    for h in range(kv_heads):
        for g in range(group):
            c = (h * group + g) * HEAD
            qa[h, g * rows : (g + 1) * rows, 0:HEAD] = q_ref[:, c : c + HEAD]
            qa[h, g * rows : (g + 1) * rows, HEAD : 2 * HEAD] = penalty

    def step(t, carry):
        now, before = place(t), place(t - LAG)
        for h in range(kv_heads):
            relay(now, h)
            attend(before, h)
        return carry

    def step_without(t, carry):
        now = place(t)
        for h in range(kv_heads):
            relay(now, h)
        return carry

    def step_own(t, carry):
        now = place(t)
        for h in range(kv_heads):
            relay(now, h)
            attend_own(h)
        return carry

    lax.fori_loop(2, LAG, step_without, 0)
    lax.fori_loop(LAG, LAG + 1, step_own, 0)
    lax.fori_loop(LAG + 1, NZ + 1, step, 0)

    loads[4].wait()
    width = group * HEAD

    def relay_out(h):
        columns = pl.ds(h * width, width)
        return pltpu.make_async_remote_copy(
            src_ref=advanced.at[:, columns],
            dst_ref=arrived_ref.at[:, columns],
            send_sem=pipe_send_sem.at[h],
            recv_sem=pipe_recv_sem.at[h],
            device_id={"pipe": following},
            device_id_type=MESH,
        )

    for h in range(kv_heads):
        across(h).wait_send()
        pass_first(h).wait_send()
        pass_second(h).wait_send()

        @pl.when(z < NZ - 1)
        def _():
            up(h).wait_send()

    def drain(t, carry):
        slot, k, onward, first_of_beyond = place(t)
        for h in range(kv_heads):

            @pl.when(onward)
            def _():
                forward_z(slot, k, h).wait_send()

            @pl.when(jnp.logical_not(first_of_beyond))
            def _():
                forward_x(slot, h).wait_send()

        return carry

    lax.fori_loop(1, NZ - LAG, drain, 0)

    squares = jnp.zeros((rows, HEAD), jnp.float32)
    for h in range(kv_heads):

        def rest(t, carry):
            attend(place(t), h)
            return carry

        lax.fori_loop(NZ - LAG + 1, NZ + 1, rest, 0)
        for g in range(group):
            c = (h * group + g) * HEAD
            top_rows = slice(g * rows, (g + 1) * rows)
            mixed = acc[h, top_rows, 0:HEAD] / acc[h, top_rows, HEAD : 2 * HEAD]
            mixed = mixed.astype(jnp.bfloat16).astype(jnp.float32)
            total = (stream_ref[:, c : c + HEAD].astype(jnp.float32) + mixed).astype(jnp.bfloat16)
            advanced[:, c : c + HEAD] = total
            wide = total.astype(jnp.float32)
            squares = squares + wide * wide
        if h < kv_heads - 1:
            relay_out(h).start()
    row_sums = jnp.broadcast_to(jnp.sum(squares, axis=1, keepdims=True), (rows, HEAD))
    square_out[...] = row_sums.T[0:8, :]

    def sums_out(t):
        return pltpu.make_async_remote_copy(
            src_ref=square_out,
            dst_ref=square_in.at[t],
            send_sem=square_send_sem.at[t],
            recv_sem=square_recv_sem.at[t],
            device_id={"pipe": following, "tp": (tp + t) % n_tp},
            device_id_type=MESH,
        )

    for t in range(n_tp):
        sums_out(n_tp - 1 - t).start()
    relay_out(kv_heads - 1).start()

    lax.fori_loop(NZ - LAG, NZ + 1, drain, 0)

    for t in range(n_tp):
        sums_out(t).wait_recv()
    total = square_in[0, 0:1, :]
    for t in range(1, n_tp):
        total = total + square_in[t, 0:1, :]
    inverse = lax.rsqrt(total / (QUERY_HEADS * HEAD) + 1e-05)
    inverse_ref[...] = jnp.broadcast_to(inverse, (rows, rows)).T
    for h in range(kv_heads):
        relay_out(h).wait_recv()
    for h in range(kv_heads):
        relay_out(h).wait_send()
    for t in range(n_tp):
        sums_out(t).wait_send()


def norm_kernel(in_ref, inverse_ref, gain_ref, arrived_ref, normed_ref):
    inverse = inverse_ref[...]
    for c in range(0, in_ref.shape[1], HEAD):
        block = in_ref[:, c : c + HEAD]
        arrived_ref[:, c : c + HEAD] = block
        gain = gain_ref[c : c + HEAD].astype(jnp.float32)[None, :]
        normed_ref[:, c : c + HEAD] = (block.astype(jnp.float32) * inverse * gain).astype(
            jnp.bfloat16
        )


def per_device(stream, queries, keys, values, segments, norm_gain):
    stream, queries, keys, values = stream[0], queries[0], keys[0], values[0]
    rows = queries.shape[0]
    kv_heads = keys.shape[1] // HEAD
    group = queries.shape[1] // keys.shape[1]
    block_rows = OH_ROWS + 2 * HEAD * kv_heads
    n_tp = lax.axis_size("tp")
    vmem = pl.BlockSpec(memory_space=pltpu.VMEM)
    anywhere = pl.BlockSpec(memory_space=pltpu.HBM)
    like_stream = jax.ShapeDtypeStruct(stream.shape, jnp.bfloat16)
    arrived, inverse = pl.pallas_call(
        functools.partial(attention_kernel, kv_heads, group),
        out_shape=(like_stream, jax.ShapeDtypeStruct((rows, HEAD), jnp.float32)),
        in_specs=[anywhere] * 5,
        out_specs=(vmem, vmem),
        scratch_shapes=[
            pltpu.VMEM(queries.shape, jnp.bfloat16),
            pltpu.VMEM(keys.shape, jnp.bfloat16),
            pltpu.VMEM(values.shape, jnp.bfloat16),
            pltpu.VMEM(stream.shape, jnp.bfloat16),
            pltpu.VMEM(segments.shape, segments.dtype),
            pltpu.VMEM(stream.shape, jnp.bfloat16),
            pltpu.VMEM((8, rows), jnp.float32),
            pltpu.VMEM((n_tp, 8, rows), jnp.float32),
            pltpu.VMEM((kv_heads, group * rows, 2 * HEAD), jnp.bfloat16),
            pltpu.VMEM((block_rows, rows), jnp.bfloat16),
            pltpu.VMEM((block_rows, rows), jnp.bfloat16),
            pltpu.VMEM((NZ, 2, block_rows, rows), jnp.bfloat16),
            pltpu.VMEM((kv_heads, group * rows, HEAD), jnp.float32),
            pltpu.VMEM((kv_heads, group * rows, 2 * HEAD), jnp.float32),
            pltpu.SemaphoreType.DMA((NZ, 2, kv_heads)),
            pltpu.SemaphoreType.DMA((NZ + 1, kv_heads)),
            pltpu.SemaphoreType.DMA((NZ + 1, kv_heads)),
            pltpu.SemaphoreType.DMA((kv_heads,)),
            pltpu.SemaphoreType.DMA((2, kv_heads)),
            pltpu.SemaphoreType.DMA((5,)),
            pltpu.SemaphoreType.DMA((kv_heads,)),
            pltpu.SemaphoreType.DMA((kv_heads,)),
            pltpu.SemaphoreType.DMA((n_tp,)),
            pltpu.SemaphoreType.DMA((n_tp,)),
        ],
        compiler_params=pltpu.CompilerParams(
            collective_id=0, has_side_effects=True, vmem_limit_bytes=63 * 1024 * 1024
        ),
    )(queries, keys, values, stream, segments)
    columns = NORM_COLUMNS
    tile = pl.BlockSpec((rows, columns), lambda i: (0, i))
    arrived, normed = pl.pallas_call(
        norm_kernel,
        grid=(stream.shape[1] // columns,),
        out_shape=(like_stream, like_stream),
        in_specs=[
            tile,
            pl.BlockSpec((rows, HEAD), lambda i: (0, 0)),
            pl.BlockSpec((columns,), lambda i: (i,)),
        ],
        out_specs=(tile, tile),
    )(arrived, inverse, norm_gain)
    return (arrived[None], normed[None])


def solution(mesh):
    in_specs = (
        P("pipe", "ctx", "tp"),
        P("pipe", "ctx", "tp"),
        P("pipe", "ctx", "tp"),
        P("pipe", "ctx", "tp"),
        P("pipe", "ctx"),
        P("tp"),
    )
    out_specs = (P("pipe", "ctx", "tp"), P("pipe", "ctx", "tp"))
    return jax.shard_map(
        per_device, mesh=mesh, in_specs=in_specs, out_specs=out_specs, check_vma=False
    )
```
